128 devices in a mesh: grp: 4 (over z), feat: 32 (over x, y, core).
Axes of the slice: x: 4, y: 4, z: 4, core: 2. Of those that a mesh axis runs over, the one named last changes fastest.
Arguments:
- features: bfloat16 [4, 768, 768, 128], P('grp', None, 'feat'), may hold values from -6 to 6
- adj_tiles: bfloat16 [4, 384, 128, 128], P('grp'), may hold values from -0.4375 to 0.4375
- tile_rows: int32 [4, 384], P('grp'), may hold values from 0 to 255, as said below
- tile_cols: int32 [4, 384], P('grp'), may hold values from 0 to 767
- self_blocks: int32 [4, 256], P('grp'), may hold values from 0 to 767, as said below
- weight: bfloat16 [1536, 1024], replicated, may hold values from -0.15625 to 0.15625
- proj_bias: float32 [1024], replicated, may hold values from -0.5 to 0.5
- cotangent: bfloat16 [4, 32768, 1024], P('grp', 'feat'), may hold values from -0.015625 to 0.015625
Outputs:
- hidden: bfloat16 [4, 32768, 1024], P('grp', 'feat')
- weight_grad: float32 [1536, 1024], P('feat')
The draws below stay inside these ranges and needn't reach their ends.
Inputs may be any that keep to these rules, and one draw needn't show every extreme that they name: `tile_rows`: within each minibatch the row blocks are in nondecreasing order and every row block 0 to 255 has at least one tile. `self_blocks`: within each minibatch the blocks are distinct.
All inputs are finite; a program needn't handle non-finite values.
Results may differ from the reference program's by a relative error of at most 0.0038.
Values may be sent and summed in bfloat16 or wider, within the bound.
No kernel may reach another device: no remote copies, remote signals or barrier semaphores. Data moves between devices by JAX's collectives and lax.ppermute only.
A program may use at most 128 MiB of HBM per device.

```python
import jax
import jax.numpy as jnp
from jax import lax

F = 768
HID = 1024
TILE = 128
GROUPS = 4
NDST = 32768
NRB = 256
NT = 384
NCB = 768


def draw_tile_rows(key, part):

    def one_group(group_key):
        key_one, key_two, key_three = jax.random.split(group_key, 3)
        extra_count = NT - NRB
        first = jax.random.randint(key_one, (extra_count,), 0, NRB)
        second = jax.random.randint(key_two, (extra_count,), 0, NRB)
        third = jax.random.randint(key_three, (extra_count,), 0, NRB)
        skewed = jnp.minimum(jnp.minimum(first, second), third).astype(jnp.int32)
        every_block = jnp.arange(NRB, dtype=jnp.int32)
        return jnp.sort(jnp.concatenate([every_block, skewed]))
    return jax.vmap(one_group)(jax.random.split(jax.random.fold_in(key, 11), GROUPS)).astype(jnp.int32)


def draw_self_blocks(key, part):

    def one_group(group_key):
        key_one, key_two = jax.random.split(group_key, 2)
        middle = jax.random.permutation(key_one, NCB - 2)[:NRB - 2].astype(jnp.int32) + 1
        ends = jnp.array([0, NCB - 1], dtype=jnp.int32)
        chosen = jnp.concatenate([middle, ends])
        order = jax.random.permutation(key_two, NRB)
        return chosen[order]
    return jax.vmap(one_group)(jax.random.split(jax.random.fold_in(key, 23), GROUPS)).astype(jnp.int32)


def with_ends(entries, rng, smallest, high):
    longest = entries.shape.index(max(entries.shape))
    spots = []
    for shift in (0, 1):
        where = [jax.random.randint(jax.random.fold_in(rng, axis), (), 0, length) for axis, length in enumerate(entries.shape)]
        where[longest] = (where[longest] + shift) % entries.shape[longest]
        spots.append(tuple(where))
    return entries.at[spots[0]].set(smallest).at[spots[1]].set(high)


def level_of(key, shape, cuts, least, high):
    loudness = 1.0
    for dim, blocks in cuts:
        heights = jax.random.uniform(jax.random.fold_in(jax.random.fold_in(key, 6), dim), (blocks,), jnp.float32, least / len(cuts), high / len(cuts))
        loudness = loudness * jnp.repeat(jnp.exp(heights), shape[dim] // blocks).reshape((-1,) + (1,) * (len(shape) - 1 - dim))
    return loudness


def noise(rng, shape, scale, bound, pieces=(), held_as=jnp.bfloat16):
    loudness = level_of(rng, shape, pieces, -0.22, 0.18) if pieces else 1.0
    result = jax.random.normal(rng, shape, jnp.float32) * scale * loudness
    return jnp.minimum(jnp.maximum(result, -bound), bound).astype(held_as)


def setup_inputs(seed: int = 0) -> dict:
    seeds = jax.random.split(jax.random.key(seed), 9)
    features = noise(seeds[0], (GROUPS, NCB, F, TILE), 1.0, 6.0, ((0, 4), (2, 32)))
    adj_tiles = noise(seeds[1], (GROUPS, NT, TILE, TILE), (TILE * NT // NRB) ** -0.5, 0.4375, ((0, 4),))
    tile_rows = draw_tile_rows(jax.random.fold_in(seeds[8], 71), 0)
    tile_cols = with_ends(jax.random.randint(seeds[3], (GROUPS, NT), 0, NCB), jax.random.fold_in(seeds[3], 1), 0, NCB - 1).astype(jnp.int32)
    self_blocks = draw_self_blocks(jax.random.fold_in(seeds[8], 71), 0)
    weight = noise(seeds[5], (2 * F, HID), (2 * F) ** -0.5, 0.15625)
    proj_bias = jnp.clip(jax.random.uniform(seeds[6], (HID,), jnp.float32, -0.5, 0.5), -0.5, 0.5)
    cotangent = noise(seeds[7], (GROUPS, NDST, HID), (GROUPS * NDST) ** -0.5, 0.015625, ((0, 4), (1, 32)))
    return dict(features=features, adj_tiles=adj_tiles, tile_rows=tile_rows, tile_cols=tile_cols, self_blocks=self_blocks, weight=weight, proj_bias=proj_bias, cotangent=cotangent)


def elu_act(value):
    return jnp.where(value > 0, value, jnp.expm1(jnp.minimum(value, 0.0)))


def combine_group(features_g, tiles_g, rows_g, cols_g, blocks_g):
    picked = jnp.take(features_g, cols_g, axis=0).astype(jnp.float32)
    contrib = jnp.einsum("tfs,tds->tfd", picked, tiles_g.astype(jnp.float32))
    summed = jax.ops.segment_sum(contrib, rows_g, num_segments=NRB)
    aggregate = summed.astype(jnp.bfloat16)
    self_feat = jnp.take(features_g, blocks_g, axis=0)
    return jnp.concatenate([self_feat, aggregate], axis=1)


def reference(features, adj_tiles, tile_rows, tile_cols, self_blocks, weight, proj_bias, cotangent):
    def step_group(carry, inputs):
        features_g, tiles_g, rows_g, cols_g, blocks_g, cot_g = inputs
        combined = combine_group(features_g, tiles_g, rows_g, cols_g, blocks_g)
        preact = jnp.einsum("rcd,ch->rdh", combined.astype(jnp.float32), weight.astype(jnp.float32))
        preact = preact.reshape(NDST, HID) + proj_bias
        hidden_g = elu_act(preact).astype(jnp.bfloat16)
        pre_grad = (cot_g.astype(jnp.float32) * jnp.exp(jnp.minimum(preact, 0.0))).astype(jnp.bfloat16)
        grad_part = jnp.einsum("rcd,rdh->ch", combined.astype(jnp.float32), pre_grad.reshape(NRB, TILE, HID).astype(jnp.float32))
        return carry + grad_part, hidden_g

    start = jnp.zeros((2 * F, HID), jnp.float32)
    weight_grad, hidden = lax.scan(step_group, start, (features, adj_tiles, tile_rows, tile_cols, self_blocks, cotangent))
    return hidden, weight_grad
```

```python
import functools

import jax
import jax.numpy as jnp
from jax import lax
from jax.experimental import pallas as pl
from jax.experimental.pallas import tpu as pltpu
from jax.sharding import Mesh, PartitionSpec as P

BF = jnp.bfloat16
F32 = jnp.float32
VMEM_LIMIT = 56 << 20


def gather_body(blocks_ref, feat_ref, out_ref, sem):
    count = out_ref.shape[0]

    def start(r, carry):
        pltpu.make_async_copy(feat_ref.at[blocks_ref[r]], out_ref.at[r], sem).start()
        return carry

    lax.fori_loop(0, count, start, 0, unroll=8)
    pltpu.make_async_copy(feat_ref.at[pl.ds(0, count)], out_ref, sem).wait()


def gather_self(blocks, feat):
    count = blocks.shape[0]
    return pl.pallas_call(
        gather_body,
        out_shape=jax.ShapeDtypeStruct((count,) + feat.shape[1:], feat.dtype),
        grid_spec=pltpu.PrefetchScalarGridSpec(
            num_scalar_prefetch=1,
            grid=(1,),
            in_specs=[pl.BlockSpec(memory_space=pl.ANY)],
            out_specs=pl.BlockSpec((count,) + feat.shape[1:], lambda i, b: (0, 0, 0)),
            scratch_shapes=[pltpu.SemaphoreType.DMA(())],
        ),
        compiler_params=pltpu.CompilerParams(vmem_limit_bytes=VMEM_LIMIT),
        name="gather_self",
    )(blocks, feat)


def aggregate_body(unroll, rows_ref, cols_ref, feat_ref, adj_ref, out_ref, acc_ref, part_ref):
    step = pl.program_id(0)
    tiles = adj_ref.shape[0]
    base = step * tiles

    @pl.when(step == 0)
    def _():
        acc_ref[...] = jnp.zeros_like(acc_ref)

    def multiply(k, carry):
        for u in range(unroll):
            local = k * unroll + u
            part_ref[local] = lax.dot_general(
                feat_ref[cols_ref[base + local]],
                adj_ref[local],
                (((1,), (1,)), ((), ())),
                preferred_element_type=F32,
            )
        return carry

    lax.fori_loop(0, tiles // unroll, multiply, 0)

    def add(k, acc):
        for u in range(unroll):
            local = k * unroll + u
            tile = base + local
            row = rows_ref[tile]
            same = jnp.logical_and(tile > 0, rows_ref[jnp.maximum(tile - 1, 0)] == row)
            keep = jnp.where(same, 1.0, 0.0).astype(F32)
            acc = part_ref[local] + acc * keep
            out_ref[row] = acc.astype(BF)
        return acc

    acc_ref[...] = lax.fori_loop(0, tiles // unroll, add, acc_ref[...])


def aggregate_tiles(rows, cols, feat, adj, nrb, steps=8, unroll=12):
    count, side, _ = adj.shape
    width = feat.shape[1]
    return pl.pallas_call(
        functools.partial(aggregate_body, unroll),
        out_shape=jax.ShapeDtypeStruct((nrb, width, side), BF),
        grid_spec=pltpu.PrefetchScalarGridSpec(
            num_scalar_prefetch=2,
            grid=(steps,),
            in_specs=[
                pl.BlockSpec(feat.shape, lambda i, a, b: (0, 0, 0), pipeline_mode=pl.Buffered(1)),
                pl.BlockSpec((count // steps, side, side), lambda i, a, b: (i, 0, 0)),
            ],
            out_specs=pl.BlockSpec((nrb, width, side), lambda i, a, b: (0, 0, 0)),
            scratch_shapes=[
                pltpu.VMEM((width, side), F32),
                pltpu.VMEM((count // steps, width, side), F32),
            ],
        ),
        compiler_params=pltpu.CompilerParams(
            vmem_limit_bytes=VMEM_LIMIT, dimension_semantics=("arbitrary",)
        ),
        name="aggregate_tiles",
    )(rows, cols, feat, adj)


def dense_body(
    core_ref, self_ref, agg_ref, weight_ref, bias_ref, cot_ref, hidden_ref, send_ref, keep_ref,
    comb_ref, grad_ref
):
    sources, own, width, side = self_ref.shape
    half = sources * width
    for r in range(own):
        cols = pl.ds(r * side, side)
        comb_ref[0:half, cols] = self_ref[:, r].reshape(half, side)
        comb_ref[half:, cols] = agg_ref[:, r].reshape(half, side)
    chunk = 4 * side
    for m in range(own // 4):
        rows = pl.ds(m * chunk, chunk)
        pre = lax.dot_general(
            comb_ref[:, rows], weight_ref[...], (((0,), (0,)), ((), ())), preferred_element_type=F32
        )
        pre = pre + bias_ref[...]
        decay = jnp.exp(jnp.minimum(pre, 0.0))
        hidden_ref[rows, :] = jnp.where(pre > 0, pre, decay - 1.0).astype(BF)
        grad_ref[rows, :] = (cot_ref[rows, :].astype(F32) * decay).astype(BF)
    core = core_ref[0]
    blocks, share, hid = send_ref.shape
    for dest, out_ref in ((1 - core, send_ref), (core, keep_ref)):
        for b in range(0, blocks, 4):
            lhs = jnp.concatenate(
                [comb_ref[pl.ds(pl.multiple_of((2 * (b + i) + dest) * share, share), share), :] for i in range(4)],
                axis=0,
            )
            part = jnp.dot(lhs, grad_ref[...], preferred_element_type=F32)
            out_ref[b:b + 4] = part.reshape(4, share, hid).astype(out_ref.dtype)


def dense_layer(core, own_self, own_agg, weight, bias, cot):
    nodes, hid = cot.shape
    channels = weight.shape[0]
    share = channels // 32
    return pl.pallas_call(
        dense_body,
        out_shape=(
            jax.ShapeDtypeStruct((nodes, hid), BF),
            jax.ShapeDtypeStruct((16, share, hid), BF),
            jax.ShapeDtypeStruct((16, share, hid), F32),
        ),
        in_specs=[pl.BlockSpec(memory_space=pltpu.SMEM)] + [pl.BlockSpec(memory_space=pltpu.VMEM)] * 5,
        out_specs=(pl.BlockSpec(memory_space=pltpu.VMEM),) * 3,
        scratch_shapes=[pltpu.VMEM((channels, nodes), BF), pltpu.VMEM((nodes, hid), BF)],
        compiler_params=pltpu.CompilerParams(vmem_limit_bytes=VMEM_LIMIT),
        name="dense_layer",
    )(core, own_self, own_agg, weight, bias, cot)


FEAT = ("x", "y", "core")


def per_device(
    features, adj_tiles, tile_rows, tile_cols, self_blocks, weight, proj_bias, cotangent
):
    feat = features[0]
    width, side = feat.shape[1:]
    nrb = self_blocks.shape[1]
    mine = gather_self(self_blocks[0], feat)
    own_self = lax.all_to_all(mine, FEAT, 0, 0, tiled=True)
    agg = aggregate_tiles(tile_rows[0], tile_cols[0], feat, adj_tiles[0], nrb)
    own_agg = lax.all_to_all(agg, FEAT, 0, 0, tiled=True)
    shape = (32, nrb // 32, width, side)
    core = lax.axis_index("core").astype(jnp.int32).reshape(1)
    hidden, send, keep = dense_layer(
        core, own_self.reshape(shape), own_agg.reshape(shape), weight, proj_bias[None], cotangent[0]
    )
    other = lax.ppermute(send, "core", [(0, 1), (1, 0)])
    pair = (keep + other.astype(F32)).astype(BF)
    pieces = lax.all_to_all(pair, ("x", "y"), 0, 0, tiled=True)
    part = jnp.sum(pieces.astype(F32), axis=0)
    totals = lax.all_gather(part, "grp", axis=0)
    return hidden[None], jnp.sum(totals, axis=0)


def solution(mesh):
    names = ("grp", "x", "y", "core")
    fine = Mesh(mesh.devices.reshape(4, 4, 4, 2), names)
    return jax.shard_map(
        per_device,
        mesh=fine,
        in_specs=(
            P("grp", None, FEAT, None),
            P("grp", None, None, None),
            P("grp", None),
            P("grp", None),
            P("grp", None),
            P(),
            P(),
            P("grp", FEAT, None),
        ),
        out_specs=(P("grp", FEAT, None), P(FEAT, None)),
        check_vma=False,
    )
```

```python
import functools

import jax
import jax.numpy as jnp
from jax import lax
from jax.experimental import pallas as pl
from jax.experimental.pallas import tpu as pltpu
from jax.sharding import Mesh, PartitionSpec as P

BF = jnp.bfloat16
F32 = jnp.float32
VMEM_LIMIT = 56 << 20


def gather_body(blocks_ref, feat_ref, out_ref, sem):
    count = out_ref.shape[0]

    def start(r, carry):
        pltpu.make_async_copy(feat_ref.at[blocks_ref[0, r]], out_ref.at[r], sem).start()
        return carry

    lax.fori_loop(0, count, start, 0, unroll=8)
    pltpu.make_async_copy(feat_ref.at[pl.ds(0, count)], out_ref, sem).wait()


def gather_self(blocks, feat):
    count = blocks.shape[1]
    return pl.pallas_call(
        gather_body,
        out_shape=jax.ShapeDtypeStruct((count,) + feat.shape[1:], feat.dtype),
        grid_spec=pltpu.PrefetchScalarGridSpec(
            num_scalar_prefetch=1,
            grid=(1,),
            in_specs=[pl.BlockSpec(memory_space=pl.ANY)],
            out_specs=pl.BlockSpec((count,) + feat.shape[1:], lambda i, b: (0, 0, 0)),
            scratch_shapes=[pltpu.SemaphoreType.DMA(())],
        ),
        compiler_params=pltpu.CompilerParams(vmem_limit_bytes=VMEM_LIMIT),
        name="gather_self",
    )(blocks, feat)


def aggregate_body(unroll, rows_ref, cols_ref, feat_ref, adj_ref, out_ref, acc_ref, part_ref):
    step = pl.program_id(0)
    tiles = adj_ref.shape[0]
    base = step * tiles

    @pl.when(step == 0)
    def _():
        acc_ref[...] = jnp.zeros_like(acc_ref)

    def multiply(k, carry):
        for u in range(unroll):
            local = k * unroll + u
            part_ref[local] = lax.dot_general(
                feat_ref[cols_ref[0, base + local]],
                adj_ref[local],
                (((1,), (1,)), ((), ())),
                preferred_element_type=F32,
            )
        return carry

    lax.fori_loop(0, tiles // unroll, multiply, 0)

    def add(k, acc):
        for u in range(unroll):
            local = k * unroll + u
            tile = base + local
            row = rows_ref[0, tile]
            same = jnp.logical_and(tile > 0, rows_ref[0, jnp.maximum(tile - 1, 0)] == row)
            keep = jnp.where(same, 1.0, 0.0).astype(F32)
            acc = part_ref[local] + acc * keep
            out_ref[row] = acc.astype(BF)
        return acc

    acc_ref[...] = lax.fori_loop(0, tiles // unroll, add, acc_ref[...])


def aggregate_tiles(rows, cols, feat, adj, nrb, steps=8, unroll=12):
    count, side, _ = adj.shape
    width = feat.shape[1]
    return pl.pallas_call(
        functools.partial(aggregate_body, unroll),
        out_shape=jax.ShapeDtypeStruct((nrb, width, side), BF),
        grid_spec=pltpu.PrefetchScalarGridSpec(
            num_scalar_prefetch=2,
            grid=(steps,),
            in_specs=[
                pl.BlockSpec(feat.shape, lambda i, a, b: (0, 0, 0), pipeline_mode=pl.Buffered(1)),
                pl.BlockSpec((count // steps, side, side), lambda i, a, b: (i, 0, 0)),
            ],
            out_specs=pl.BlockSpec((nrb, width, side), lambda i, a, b: (0, 0, 0)),
            scratch_shapes=[
                pltpu.VMEM((width, side), F32),
                pltpu.VMEM((count // steps, width, side), F32),
            ],
        ),
        compiler_params=pltpu.CompilerParams(
            vmem_limit_bytes=VMEM_LIMIT, dimension_semantics=("arbitrary",)
        ),
        cost_estimate=pl.CostEstimate(
            flops=2 * count * width * side * side,
            transcendentals=0,
            bytes_accessed=2 * (feat.size + adj.size + nrb * width * side),
        ),
        name="aggregate_tiles",
    )(rows, cols, feat, adj)


def dense_body(
    place_ref, self_ref, agg_ref, weight_ref, bias_ref, cot_ref,
    hidden_ref, send0_ref, send1_ref, keep0_ref, keep1_ref, comb_ref, grad_ref,
):
    sources, own, width, side = self_ref.shape
    half = sources * width
    for r in range(own):
        cols = pl.ds(r * side, side)
        comb_ref[0:half, cols] = self_ref[:, r].reshape(half, side)
        comb_ref[half:, cols] = agg_ref[:, r].reshape(half, side)
    chunk = 4 * side
    for m in range(own // 4):
        rows = pl.ds(m * chunk, chunk)
        pre = lax.dot_general(
            comb_ref[:, rows], weight_ref[...], (((0,), (0,)), ((), ())), preferred_element_type=F32
        )
        pre = pre + bias_ref[...]
        decay = jnp.exp(jnp.minimum(pre, 0.0))
        hidden_ref[rows, :] = jnp.where(pre > 0, pre, decay - 1.0).astype(BF)
        grad_ref[rows, :] = (cot_ref[rows, :].astype(F32) * decay).astype(BF)
    x, y, core = place_ref[0], place_ref[1], place_ref[2]
    hid = cot_ref.shape[1]
    share = comb_ref.shape[0] // 32

    def block(dx, dy, dest):
        first = (8 * ((x + dx) % 4) + 2 * ((y + dy) % 4) + dest) * share
        return comb_ref[pl.ds(pl.multiple_of(first, share), share), :]

    outs = ((send0_ref, send1_ref), (keep0_ref, keep1_ref))
    for dest, refs in zip((1 - core, core), outs):
        for part in range(2):
            pairs = [(k, j) if part == 0 else (j, k) for k in range(4) for j in range(4)]
            lhs = jnp.concatenate([block(dx, dy, dest) for dx, dy in pairs], axis=0)
            cols = pl.ds(part * (hid // 2), hid // 2)
            total = jnp.dot(lhs, grad_ref[:, cols], preferred_element_type=F32)
            refs[part][...] = total.reshape(refs[part].shape).astype(refs[part].dtype)


def dense_layer(place, own_self, own_agg, weight, bias, cot):
    nodes, hid = cot.shape
    channels = weight.shape[0]
    piece = (4, channels // 8, hid // 2)
    vmem = pl.BlockSpec(memory_space=pltpu.VMEM)
    return pl.pallas_call(
        dense_body,
        out_shape=(
            jax.ShapeDtypeStruct((nodes, hid), BF),
            jax.ShapeDtypeStruct(piece, BF),
            jax.ShapeDtypeStruct(piece, BF),
            jax.ShapeDtypeStruct(piece, F32),
            jax.ShapeDtypeStruct(piece, F32),
        ),
        in_specs=[pl.BlockSpec(memory_space=pltpu.SMEM)] + [vmem] * 5,
        out_specs=(vmem,) * 5,
        scratch_shapes=[pltpu.VMEM((channels, nodes), BF), pltpu.VMEM((nodes, hid), BF)],
        compiler_params=pltpu.CompilerParams(vmem_limit_bytes=VMEM_LIMIT),
        name="dense_layer",
    )(place, own_self, own_agg, weight, bias, cot)


def shift(value, axis, k):
    return lax.ppermute(value, axis, [(i, (i + k) % 4) for i in range(4)])


def exchange(parts, axis):
    total = parts[0].astype(F32)
    for k in (1, 2, 3):
        total = total + shift(parts[k].astype(BF), axis, k).astype(F32)
    return total


FEAT = ("x", "y", "core")


def per_device(
    features, adj_tiles, tile_rows, tile_cols, self_blocks, weight, proj_bias, cotangent
):
    feat = features[0]
    width, side = feat.shape[1:]
    nrb = self_blocks.shape[1]
    mine = gather_self(self_blocks, feat)
    feat, mine = lax.optimization_barrier((feat, mine))
    own_self = lax.all_to_all(mine, FEAT, 0, 0, tiled=True)
    agg = aggregate_tiles(tile_rows, tile_cols, feat, adj_tiles[0], nrb)
    own_agg = lax.all_to_all(agg, FEAT, 0, 0, tiled=True)
    shape = (32, nrb // 32, width, side)
    place = jnp.stack([lax.axis_index(a) for a in FEAT]).astype(jnp.int32)
    hidden, send0, send1, keep0, keep1 = dense_layer(
        place, own_self.reshape(shape), own_agg.reshape(shape), weight, proj_bias[None], cotangent[0]
    )
    share, half = weight.shape[0] // 32, weight.shape[1] // 2
    swap = [(0, 1), (1, 0)]
    totals = []
    for send, keep, first, second in ((send0, keep0, "x", "y"), (send1, keep1, "y", "x")):
        pair = keep + lax.ppermute(send, "core", swap).astype(F32)
        once = exchange([pair[k] for k in range(4)], first).reshape(4, share, half)
        totals.append(exchange([once[k] for k in range(4)], second))
    mine = jnp.concatenate(totals, axis=1).astype(BF)
    n1, n2, n3 = (shift(mine, "grp", -k).astype(F32) for k in (1, 2, 3))
    odd = lax.axis_index("grp") % 2 == 1
    total = (mine.astype(F32) + jnp.where(odd, n3, n1)) + (n2 + jnp.where(odd, n1, n3))
    return hidden[None], total


def solution(mesh):
    names = ("grp", "x", "y", "core")
    fine = Mesh(mesh.devices.reshape(4, 4, 4, 2), names)
    return jax.shard_map(
        per_device,
        mesh=fine,
        in_specs=(
            P("grp", None, FEAT, None),
            P("grp", None, None, None),
            P("grp", None),
            P("grp", None),
            P("grp", None),
            P(),
            P(),
            P("grp", FEAT, None),
        ),
        out_specs=(P("grp", FEAT, None), P(FEAT, None)),
        check_vma=False,
    )
```

```python
import functools

import jax
import jax.numpy as jnp
from jax import lax
from jax.experimental import pallas as pl
from jax.experimental.pallas import tpu as pltpu
from jax.sharding import Mesh, PartitionSpec as P

BF = jnp.bfloat16
F32 = jnp.float32
MIB = 1 << 20


def in_vmem(value):
    return pltpu.with_memory_space_constraint(value, pltpu.VMEM)


def in_hbm(value):
    return pltpu.with_memory_space_constraint(value, pltpu.HBM)


def gather_body(blocks_ref, feat_ref, out_ref, sem):
    count = out_ref.shape[0]

    def start(r, carry):
        pltpu.make_async_copy(feat_ref.at[blocks_ref[0, r]], out_ref.at[r], sem).start()
        return carry

    lax.fori_loop(0, count, start, 0, unroll=8)
    pltpu.make_async_copy(feat_ref.at[pl.ds(0, count)], out_ref, sem).wait()


def gather_self(blocks, feat):
    count = blocks.shape[1]
    return pl.pallas_call(
        gather_body,
        out_shape=jax.ShapeDtypeStruct((count,) + feat.shape[1:], feat.dtype),
        grid_spec=pltpu.PrefetchScalarGridSpec(
            num_scalar_prefetch=1,
            grid=(1,),
            in_specs=[pl.BlockSpec(memory_space=pl.ANY)],
            out_specs=pl.BlockSpec((count,) + feat.shape[1:], lambda i, b: (0, 0, 0)),
            scratch_shapes=[pltpu.SemaphoreType.DMA(())],
        ),
        compiler_params=pltpu.CompilerParams(vmem_limit_bytes=56 * MIB),
        name="gather_self",
    )(blocks, feat)


def aggregate_body(unroll, rows_ref, cols_ref, feat_ref, adj_ref, out_ref, acc_ref, part_ref):
    step = pl.program_id(0)
    tiles = adj_ref.shape[0]
    base = step * tiles

    @pl.when(step == 0)
    def _():
        acc_ref[...] = jnp.zeros_like(acc_ref)

    def multiply(k, carry):
        for u in range(unroll):
            local = k * unroll + u
            part_ref[local] = lax.dot_general(
                feat_ref[cols_ref[0, base + local]],
                adj_ref[local],
                (((1,), (1,)), ((), ())),
                preferred_element_type=F32,
            )
        return carry

    lax.fori_loop(0, tiles // unroll, multiply, 0)

    def add(k, acc):
        for u in range(unroll):
            local = k * unroll + u
            tile = base + local
            row = rows_ref[0, tile]
            same = jnp.logical_and(tile > 0, rows_ref[0, jnp.maximum(tile - 1, 0)] == row)
            keep = jnp.where(same, 1.0, 0.0).astype(F32)
            acc = part_ref[local] + acc * keep
            out_ref[row] = acc.astype(BF)
        return acc

    acc_ref[...] = lax.fori_loop(0, tiles // unroll, add, acc_ref[...])


def aggregate_tiles(rows, cols, feat, adj, nrb, steps=8, unroll=12):
    count, side, _ = adj.shape
    width = feat.shape[1]
    return pl.pallas_call(
        functools.partial(aggregate_body, unroll),
        out_shape=jax.ShapeDtypeStruct((nrb, width, side), BF),
        grid_spec=pltpu.PrefetchScalarGridSpec(
            num_scalar_prefetch=2,
            grid=(steps,),
            in_specs=[
                pl.BlockSpec(feat.shape, lambda i, a, b: (0, 0, 0), pipeline_mode=pl.Buffered(1)),
                pl.BlockSpec((count // steps, side, side), lambda i, a, b: (i, 0, 0)),
            ],
            out_specs=pl.BlockSpec((nrb, width, side), lambda i, a, b: (0, 0, 0)),
            scratch_shapes=[
                pltpu.VMEM((width, side), F32),
                pltpu.VMEM((count // steps, width, side), F32),
            ],
        ),
        compiler_params=pltpu.CompilerParams(
            vmem_limit_bytes=56 * MIB, dimension_semantics=("arbitrary",)
        ),
        cost_estimate=pl.CostEstimate(
            flops=2 * count * width * side * side,
            transcendentals=0,
            bytes_accessed=2 * (feat.size + adj.size + nrb * width * side),
        ),
        name="aggregate_tiles",
    )(rows, cols, feat, adj)


def stack_channels(own_ref, comb_ref):
    sources, own, width, side = own_ref.shape
    for r in range(own):
        comb_ref[:, pl.ds(r * side, side)] = own_ref[:, r].reshape(sources * width, side)


def dense_self_body(self_ref, weight_ref, bias_ref, comb_ref, pre_ref):
    stack_channels(self_ref, comb_ref)
    half, nodes = comb_ref.shape
    chunk = nodes // 2
    for m in range(2):
        rows = pl.ds(m * chunk, chunk)
        pre = lax.dot_general(
            comb_ref[:, rows], weight_ref[:half, :], (((0,), (0,)), ((), ())), preferred_element_type=F32
        )
        pre_ref[rows, :] = pre + bias_ref[...]


def dense_self(own_self, weight, bias):
    sources, own, width, side = own_self.shape
    vmem = pl.BlockSpec(memory_space=pltpu.VMEM)
    return pl.pallas_call(
        dense_self_body,
        out_shape=(
            pltpu.HBM((sources * width, own * side), BF),
            pltpu.HBM((own * side, weight.shape[1]), F32),
        ),
        in_specs=[vmem] * 3,
        out_specs=(vmem,) * 2,
        compiler_params=pltpu.CompilerParams(vmem_limit_bytes=56 * MIB),
        name="dense_self",
    )(in_vmem(own_self), in_hbm(weight), in_hbm(bias))


def dense_rest_body(
    core_ref, agg_ref, comb_self_hbm, pre_hbm, weight_hbm, cot_hbm,
    hidden_hbm, send_ref, keep_ref,
    comb_ref, grad_ref, hidden_ref, comb_self_ref, pre_ref, weight_ref, cot_ref, sem,
):
    half, nodes = comb_ref.shape
    chunk = nodes // 2
    chunks = [pl.ds(m * chunk, chunk) for m in range(2)]
    sources = [(weight_hbm.at[pl.ds(half, half)], weight_ref)]
    for rows in chunks:
        sources.append((pre_hbm.at[rows], pre_ref.at[rows]))
        sources.append((cot_hbm.at[rows], cot_ref.at[rows]))
    sources.append((comb_self_hbm, comb_self_ref))
    loads = [pltpu.make_async_copy(a, b, sem.at[i]) for i, (a, b) in enumerate(sources)]
    for load in loads:
        load.start()
    stack_channels(agg_ref, comb_ref)
    loads[0].wait()
    stores = []
    for m, rows in enumerate(chunks):
        part = lax.dot_general(
            comb_ref[:, rows], weight_ref[...], (((0,), (0,)), ((), ())), preferred_element_type=F32
        )
        loads[1 + 2 * m].wait()
        loads[2 + 2 * m].wait()
        pre = pre_ref[rows, :] + part
        decay = jnp.exp(jnp.minimum(pre, 0.0))
        hidden_ref[rows, :] = jnp.where(pre > 0, pre, decay - 1.0).astype(BF)
        grad_ref[rows, :] = (cot_ref[rows, :].astype(F32) * decay).astype(BF)
        stores.append(pltpu.make_async_copy(hidden_ref.at[rows], hidden_hbm.at[rows], sem.at[6 + m]))
        stores[m].start()
    loads[5].wait()
    core = core_ref[0]
    zs, blocks, share, width = send_ref.shape
    for dest, out_ref in ((1 - core, send_ref), (core, keep_ref)):
        lhs = jnp.concatenate(
            [
                source[pl.ds(pl.multiple_of((2 * b + dest) * share, share), share), :]
                for source in (comb_self_ref, comb_ref)
                for b in range(blocks // 2)
            ],
            axis=0,
        )
        for z in range(zs):
            total = jnp.dot(lhs, grad_ref[:, pl.ds(z * width, width)], preferred_element_type=F32)
            out_ref[z] = total.reshape(blocks, share, width).astype(out_ref.dtype)
    for store in stores:
        store.wait()


def dense_rest(core, own_agg, comb_self, pre, weight, cot):
    nodes, hid = cot.shape
    half = comb_self.shape[0]
    pieces = (4, 16, half // 16, hid // 4)
    vmem = pl.BlockSpec(memory_space=pltpu.VMEM)
    return pl.pallas_call(
        dense_rest_body,
        out_shape=(
            jax.ShapeDtypeStruct((nodes, hid), BF),
            pltpu.VMEM(pieces, BF),
            pltpu.VMEM(pieces, F32),
        ),
        in_specs=[pl.BlockSpec(memory_space=pltpu.SMEM), vmem]
        + [pl.BlockSpec(memory_space=pl.ANY)] * 4,
        out_specs=(pl.BlockSpec(memory_space=pl.ANY), vmem, vmem),
        scratch_shapes=[
            pltpu.VMEM((half, nodes), BF),
            pltpu.VMEM((nodes, hid), BF),
            pltpu.VMEM((nodes, hid), BF),
            pltpu.VMEM((half, nodes), BF),
            pltpu.VMEM((nodes, hid), F32),
            pltpu.VMEM((half, hid), BF),
            pltpu.VMEM((nodes, hid), BF),
            pltpu.SemaphoreType.DMA((8,)),
        ],
        compiler_params=pltpu.CompilerParams(vmem_limit_bytes=32 * MIB),
        name="dense_rest",
    )(core, in_vmem(own_agg), *map(in_hbm, (comb_self, pre, weight, cot)))


def shift(value, axis, k):
    return lax.ppermute(value, axis, [(i, (i + k) % 4) for i in range(4)])


FEAT = ("x", "y", "core")


def per_device(
    features, adj_tiles, tile_rows, tile_cols, self_blocks, weight, proj_bias, cotangent
):
    feat = features[0]
    width, side = feat.shape[1:]
    nrb = self_blocks.shape[1]
    mine = gather_self(self_blocks, feat)
    feat, mine = lax.optimization_barrier((feat, mine))
    own_self = lax.all_to_all(mine, FEAT, 0, 0, tiled=True)
    agg = aggregate_tiles(tile_rows, tile_cols, feat, adj_tiles[0], nrb)
    own_agg = lax.all_to_all(agg, FEAT, 0, 0, tiled=True)
    shape = (32, nrb // 32, width, side)
    comb_self, pre = dense_self(own_self.reshape(shape), weight, proj_bias[None])
    core = lax.axis_index("core").astype(jnp.int32).reshape(1)
    hidden, send, keep = dense_rest(
        core, own_agg.reshape(shape), comb_self, pre, weight, cotangent[0]
    )
    pair = (keep + lax.ppermute(send, "core", [(0, 1), (1, 0)]).astype(F32)).astype(BF)
    pair = pair.reshape((64,) + pair.shape[2:])
    pieces = lax.all_to_all(pair, ("grp", "x", "y"), 0, 0, tiled=True)
    piece = jnp.sum(pieces.astype(F32), axis=0)
    near = [piece] + [shift(piece, "grp", -k) for k in (1, 2, 3)]
    grp = lax.axis_index("grp")
    columns = []
    for z in range(4):
        k = (z - grp) % 4
        columns.append(
            jnp.where(k == 0, near[0], jnp.where(k == 1, near[1], jnp.where(k == 2, near[2], near[3])))
        )
    return hidden[None], jnp.concatenate(columns, axis=1)


def solution(mesh):
    names = ("grp", "x", "y", "core")
    fine = Mesh(mesh.devices.reshape(4, 4, 4, 2), names)
    return jax.shard_map(
        per_device,
        mesh=fine,
        in_specs=(
            P("grp", None, FEAT, None),
            P("grp", None, None, None),
            P("grp", None),
            P("grp", None),
            P("grp", None),
            P(),
            P(),
            P("grp", FEAT, None),
        ),
        out_specs=(P("grp", FEAT, None), P(FEAT, None)),
        check_vma=False,
    )
```

```python
import functools

import jax
import jax.numpy as jnp
from jax import lax
from jax.experimental import pallas as pl
from jax.experimental.pallas import tpu as pltpu
from jax.sharding import Mesh, PartitionSpec as P

BF = jnp.bfloat16
F32 = jnp.float32
MIB = 1 << 20


def in_vmem(value):
    return pltpu.with_memory_space_constraint(value, pltpu.VMEM)


def in_hbm(value):
    return pltpu.with_memory_space_constraint(value, pltpu.HBM)


def gather_body(blocks_ref, feat_ref, out_ref, sem):
    count = out_ref.shape[0]

    def start(r, carry):
        pltpu.make_async_copy(feat_ref.at[blocks_ref[0, r]], out_ref.at[r], sem).start()
        return carry

    lax.fori_loop(0, count, start, 0, unroll=8)
    pltpu.make_async_copy(feat_ref.at[pl.ds(0, count)], out_ref, sem).wait()


def gather_self(blocks, feat):
    count = blocks.shape[1]
    return pl.pallas_call(
        gather_body,
        out_shape=jax.ShapeDtypeStruct((count,) + feat.shape[1:], feat.dtype),
        grid_spec=pltpu.PrefetchScalarGridSpec(
            num_scalar_prefetch=1,
            grid=(1,),
            in_specs=[pl.BlockSpec(memory_space=pl.ANY)],
            out_specs=pl.BlockSpec(memory_space=pl.ANY),
            scratch_shapes=[pltpu.SemaphoreType.DMA(())],
        ),
        compiler_params=pltpu.CompilerParams(vmem_limit_bytes=56 * MIB),
        name="gather_self",
    )(blocks, feat)


def aggregate_body(unroll, rows_ref, cols_ref, feat_ref, adj_ref, out_ref, acc_ref, part_ref):
    step = pl.program_id(0)
    tiles = adj_ref.shape[0]
    base = step * tiles

    @pl.when(step == 0)
    def _():
        acc_ref[...] = jnp.zeros_like(acc_ref)

    def multiply(k, carry):
        for u in range(unroll):
            local = k * unroll + u
            part_ref[local] = lax.dot_general(
                feat_ref[cols_ref[0, base + local]],
                adj_ref[local],
                (((1,), (1,)), ((), ())),
                preferred_element_type=F32,
            )
        return carry

    lax.fori_loop(0, tiles // unroll, multiply, 0)

    def add(k, acc):
        for u in range(unroll):
            local = k * unroll + u
            tile = base + local
            row = rows_ref[0, tile]
            same = jnp.logical_and(tile > 0, rows_ref[0, jnp.maximum(tile - 1, 0)] == row)
            keep = jnp.where(same, 1.0, 0.0).astype(F32)
            acc = part_ref[local] + acc * keep
            out_ref[row] = acc.astype(BF)
        return acc

    acc_ref[...] = lax.fori_loop(0, tiles // unroll, add, acc_ref[...])


def aggregate_tiles(rows, cols, feat, adj, nrb, steps=8, unroll=12):
    count, side, _ = adj.shape
    width = feat.shape[1]
    return pl.pallas_call(
        functools.partial(aggregate_body, unroll),
        out_shape=jax.ShapeDtypeStruct((nrb, width, side), BF),
        grid_spec=pltpu.PrefetchScalarGridSpec(
            num_scalar_prefetch=2,
            grid=(steps,),
            in_specs=[
                pl.BlockSpec(feat.shape, lambda i, a, b: (0, 0, 0), pipeline_mode=pl.Buffered(1)),
                pl.BlockSpec((count // steps, side, side), lambda i, a, b: (i, 0, 0)),
            ],
            out_specs=pl.BlockSpec((nrb, width, side), lambda i, a, b: (0, 0, 0)),
            scratch_shapes=[
                pltpu.VMEM((width, side), F32),
                pltpu.VMEM((count // steps, width, side), F32),
            ],
        ),
        compiler_params=pltpu.CompilerParams(
            vmem_limit_bytes=56 * MIB, dimension_semantics=("arbitrary",)
        ),
        cost_estimate=pl.CostEstimate(
            flops=2 * count * width * side * side,
            transcendentals=0,
            bytes_accessed=2 * (feat.size + adj.size + nrb * width * side),
        ),
        name="aggregate_tiles",
    )(rows, cols, feat, adj)


def stack_channels(own_ref, comb_ref):
    sources, own, width, side = own_ref.shape
    for r in range(own):
        comb_ref[:, pl.ds(r * side, side)] = own_ref[:, r].reshape(sources * width, side)


def dense_self_body(self_ref, weight_ref, bias_ref, comb_ref, pre_ref):
    stack_channels(self_ref, comb_ref)
    half, nodes = comb_ref.shape
    chunk = nodes // 2
    for m in range(2):
        rows = pl.ds(m * chunk, chunk)
        pre = lax.dot_general(
            comb_ref[:, rows], weight_ref[:half, :], (((0,), (0,)), ((), ())), preferred_element_type=F32
        )
        pre_ref[rows, :] = pre + bias_ref[...]


def dense_self(own_self, weight, bias):
    sources, own, width, side = own_self.shape
    vmem = pl.BlockSpec(memory_space=pltpu.VMEM)
    return pl.pallas_call(
        dense_self_body,
        out_shape=(
            pltpu.HBM((sources * width, own * side), BF),
            pltpu.HBM((own * side, weight.shape[1]), F32),
        ),
        in_specs=[vmem] * 3,
        out_specs=(vmem,) * 2,
        compiler_params=pltpu.CompilerParams(vmem_limit_bytes=56 * MIB),
        name="dense_self",
    )(in_vmem(own_self), in_hbm(weight), in_hbm(bias))


def dense_rest_body(
    core_ref, agg_ref, comb_self_hbm, pre_hbm, weight_hbm, cot_hbm,
    total_hbm, comb_ref, grad_ref, send_ref,
    comb_self_ref, pre_ref, weight_ref, cot_ref, sem,
):
    half, nodes = comb_ref.shape
    chunk = nodes // 2
    chunks = [pl.ds(m * chunk, chunk) for m in range(2)]
    sources = [(weight_hbm.at[pl.ds(half, half)], weight_ref)]
    for rows in chunks:
        sources.append((pre_hbm.at[rows], pre_ref.at[rows]))
        sources.append((cot_hbm.at[rows], cot_ref.at[rows]))
    sources.append((comb_self_hbm, comb_self_ref))
    loads = [pltpu.make_async_copy(a, b, sem.at[i]) for i, (a, b) in enumerate(sources)]
    for load in loads:
        load.start()
    stack_channels(agg_ref, comb_ref)
    loads[0].wait()
    stores = []
    for m, rows in enumerate(chunks):
        part = lax.dot_general(
            comb_ref[:, rows], weight_ref[...], (((0,), (0,)), ((), ())), preferred_element_type=F32
        )
        loads[1 + 2 * m].wait()
        loads[2 + 2 * m].wait()
        pre = pre_ref[rows, :] + part
        pre_ref[rows, :] = pre
        stores.append(pltpu.make_async_copy(pre_ref.at[rows], total_hbm.at[rows], sem.at[6 + m]))
        stores[m].start()
        grad_ref[rows, :] = (cot_ref[rows, :].astype(F32) * jnp.exp(jnp.minimum(pre, 0.0))).astype(BF)
    loads[5].wait()
    weight_terms(1 - core_ref[0], comb_self_ref, comb_ref, grad_ref, send_ref)
    for store in stores:
        store.wait()


def weight_terms(dest, comb_self_ref, comb_ref, grad_ref, out_ref):
    zs, blocks, share, width = out_ref.shape
    lhs = jnp.concatenate(
        [
            source[pl.ds(pl.multiple_of((2 * b + dest) * share, share), share), :]
            for source in (comb_self_ref, comb_ref)
            for b in range(blocks // 2)
        ],
        axis=0,
    )
    for z in range(zs):
        total = jnp.dot(lhs, grad_ref[:, pl.ds(z * width, width)], preferred_element_type=F32)
        out_ref[z] = total.reshape(blocks, share, width).astype(out_ref.dtype)


def pieces_of(half, hid):
    return (4, 16, half // 16, hid // 4)


def dense_rest(core, own_agg, comb_self, pre, weight, cot):
    nodes, hid = cot.shape
    half = comb_self.shape[0]
    vmem = pl.BlockSpec(memory_space=pltpu.VMEM)
    return pl.pallas_call(
        dense_rest_body,
        out_shape=(
            pltpu.HBM((nodes, hid), F32),
            pltpu.VMEM((half, nodes), BF),
            pltpu.VMEM((nodes, hid), BF),
            pltpu.VMEM(pieces_of(half, hid), BF),
        ),
        in_specs=[pl.BlockSpec(memory_space=pltpu.SMEM), vmem]
        + [pl.BlockSpec(memory_space=pl.ANY)] * 4,
        out_specs=(pl.BlockSpec(memory_space=pl.ANY),) + (vmem,) * 3,
        scratch_shapes=[
            pltpu.VMEM((half, nodes), BF),
            pltpu.VMEM((nodes, hid), F32),
            pltpu.VMEM((half, hid), BF),
            pltpu.VMEM((nodes, hid), BF),
            pltpu.SemaphoreType.DMA((8,)),
        ],
        compiler_params=pltpu.CompilerParams(vmem_limit_bytes=24 * MIB),
        name="dense_rest",
    )(core, in_vmem(own_agg), *map(in_hbm, (comb_self, pre, weight, cot)))


def dense_keep_body(core_ref, comb_self_hbm, comb_ref, grad_ref, keep_ref, comb_self_ref, sem):
    load = pltpu.make_async_copy(comb_self_hbm, comb_self_ref, sem)
    load.start()
    load.wait()
    weight_terms(core_ref[0], comb_self_ref, comb_ref, grad_ref, keep_ref)


def dense_keep(core, comb_self, comb_agg, grad):
    half, nodes = comb_self.shape
    hid = grad.shape[1]
    vmem = pl.BlockSpec(memory_space=pltpu.VMEM)
    return pl.pallas_call(
        dense_keep_body,
        out_shape=pltpu.VMEM(pieces_of(half, hid), F32),
        in_specs=[pl.BlockSpec(memory_space=pltpu.SMEM), pl.BlockSpec(memory_space=pl.ANY), vmem, vmem],
        out_specs=vmem,
        scratch_shapes=[pltpu.VMEM((half, nodes), BF), pltpu.SemaphoreType.DMA(())],
        compiler_params=pltpu.CompilerParams(vmem_limit_bytes=16 * MIB),
        name="dense_keep",
    )(core, in_hbm(comb_self), in_vmem(comb_agg), in_vmem(grad))


def shift(value, axis, k):
    return lax.ppermute(value, axis, [(i, (i + k) % 4) for i in range(4)])


FEAT = ("x", "y", "core")


def per_device(
    features, adj_tiles, tile_rows, tile_cols, self_blocks, weight, proj_bias, cotangent
):
    feat = features[0]
    width, side = feat.shape[1:]
    nrb = self_blocks.shape[1]
    mine = gather_self(self_blocks, feat)
    feat, mine = lax.optimization_barrier((feat, mine))
    own_self = lax.all_to_all(mine, FEAT, 0, 0, tiled=True)
    agg = aggregate_tiles(tile_rows, tile_cols, feat, adj_tiles[0], nrb)
    own_agg = lax.all_to_all(agg, FEAT, 0, 0, tiled=True)
    shape = (32, nrb // 32, width, side)
    comb_self, pre = dense_self(own_self.reshape(shape), weight, proj_bias[None])
    core = lax.axis_index("core").astype(jnp.int32).reshape(1)
    pre, comb_agg, grad, send = dense_rest(
        core, own_agg.reshape(shape), comb_self, pre, weight, cotangent[0]
    )
    other = lax.ppermute(send, "core", [(0, 1), (1, 0)])
    keep = dense_keep(core, comb_self, comb_agg, grad)
    hidden = jnp.where(pre > 0, pre, jnp.exp(jnp.minimum(pre, 0.0)) - 1.0).astype(BF)
    pair = (keep + other.astype(F32)).astype(BF)
    pair = pair.reshape((64,) + pair.shape[2:])
    pieces = lax.all_to_all(pair, ("grp", "x", "y"), 0, 0, tiled=True)
    piece = jnp.sum(pieces.astype(F32), axis=0)
    near = [piece] + [shift(piece, "grp", -k) for k in (1, 2, 3)]
    grp = lax.axis_index("grp")
    columns = []
    for z in range(4):
        k = (z - grp) % 4
        columns.append(
            jnp.where(k == 0, near[0], jnp.where(k == 1, near[1], jnp.where(k == 2, near[2], near[3])))
        )
    return hidden[None], jnp.concatenate(columns, axis=1)


def solution(mesh):
    names = ("grp", "x", "y", "core")
    fine = Mesh(mesh.devices.reshape(4, 4, 4, 2), names)
    return jax.shard_map(
        per_device,
        mesh=fine,
        in_specs=(
            P("grp", None, FEAT, None),
            P("grp", None, None, None),
            P("grp", None),
            P("grp", None),
            P("grp", None),
            P(),
            P(),
            P("grp", FEAT, None),
        ),
        out_specs=(P("grp", FEAT, None), P(FEAT, None)),
        check_vma=False,
    )
```

```python
import functools

import jax
import jax.numpy as jnp
from jax import lax
from jax.experimental import pallas as pl
from jax.experimental.pallas import tpu as pltpu
from jax.sharding import Mesh, PartitionSpec as P

BF = jnp.bfloat16
F32 = jnp.float32
MIB = 1 << 20


def in_vmem(value):
    return pltpu.with_memory_space_constraint(value, pltpu.VMEM)


def in_hbm(value):
    return pltpu.with_memory_space_constraint(value, pltpu.HBM)


def gather_body(blocks_ref, feat_ref, out_ref, sem):
    count = out_ref.shape[0]

    def start(r, carry):
        pltpu.make_async_copy(feat_ref.at[blocks_ref[0, r]], out_ref.at[r], sem).start()
        return carry

    lax.fori_loop(0, count, start, 0, unroll=8)
    pltpu.make_async_copy(feat_ref.at[pl.ds(0, count)], out_ref, sem).wait()


def gather_self(blocks, feat):
    count = blocks.shape[1]
    return pl.pallas_call(
        gather_body,
        out_shape=jax.ShapeDtypeStruct((count,) + feat.shape[1:], feat.dtype),
        grid_spec=pltpu.PrefetchScalarGridSpec(
            num_scalar_prefetch=1,
            grid=(1,),
            in_specs=[pl.BlockSpec(memory_space=pl.ANY)],
            out_specs=pl.BlockSpec((count,) + feat.shape[1:], lambda i, b: (0, 0, 0)),
            scratch_shapes=[pltpu.SemaphoreType.DMA(())],
        ),
        compiler_params=pltpu.CompilerParams(vmem_limit_bytes=56 * MIB),
        name="gather_self",
    )(blocks, feat)


def aggregate_body(unroll, rows_ref, cols_ref, feat_ref, adj_ref, out_ref, acc_ref, part_ref):
    step = pl.program_id(0)
    tiles = adj_ref.shape[0]
    base = step * tiles

    @pl.when(step == 0)
    def _():
        acc_ref[...] = jnp.zeros_like(acc_ref)

    def multiply(k, carry):
        for u in range(unroll):
            local = k * unroll + u
            part_ref[local] = lax.dot_general(
                feat_ref[cols_ref[0, base + local]],
                adj_ref[local],
                (((1,), (1,)), ((), ())),
                preferred_element_type=F32,
            )
        return carry

    lax.fori_loop(0, tiles // unroll, multiply, 0)

    def add(k, acc):
        for u in range(unroll):
            local = k * unroll + u
            tile = base + local
            row = rows_ref[0, tile]
            same = jnp.logical_and(tile > 0, rows_ref[0, jnp.maximum(tile - 1, 0)] == row)
            keep = jnp.where(same, 1.0, 0.0).astype(F32)
            acc = part_ref[local] + acc * keep
            out_ref[row] = acc.astype(BF)
        return acc

    acc_ref[...] = lax.fori_loop(0, tiles // unroll, add, acc_ref[...])


def aggregate_tiles(rows, cols, feat, adj, nrb, steps=8, unroll=12):
    count, side, _ = adj.shape
    width = feat.shape[1]
    return pl.pallas_call(
        functools.partial(aggregate_body, unroll),
        out_shape=jax.ShapeDtypeStruct((nrb, width, side), BF),
        grid_spec=pltpu.PrefetchScalarGridSpec(
            num_scalar_prefetch=2,
            grid=(steps,),
            in_specs=[
                pl.BlockSpec(feat.shape, lambda i, a, b: (0, 0, 0), pipeline_mode=pl.Buffered(1)),
                pl.BlockSpec((count // steps, side, side), lambda i, a, b: (i, 0, 0)),
            ],
            out_specs=pl.BlockSpec((nrb, width, side), lambda i, a, b: (0, 0, 0)),
            scratch_shapes=[
                pltpu.VMEM((width, side), F32),
                pltpu.VMEM((count // steps, width, side), F32),
            ],
        ),
        compiler_params=pltpu.CompilerParams(
            vmem_limit_bytes=56 * MIB, dimension_semantics=("arbitrary",)
        ),
        cost_estimate=pl.CostEstimate(
            flops=2 * count * width * side * side,
            transcendentals=0,
            bytes_accessed=2 * (feat.size + adj.size + nrb * width * side),
        ),
        name="aggregate_tiles",
    )(rows, cols, feat, adj)


def stack_channels(own_ref, comb_ref):
    sources, own, width, side = own_ref.shape
    for r in range(own):
        comb_ref[:, pl.ds(r * side, side)] = own_ref[:, r].reshape(sources * width, side)


def dense_self_body(self_ref, weight_ref, bias_ref, comb_ref, pre_ref):
    stack_channels(self_ref, comb_ref)
    half, nodes = comb_ref.shape
    chunk = nodes // 2
    for m in range(2):
        rows = pl.ds(m * chunk, chunk)
        pre = lax.dot_general(
            comb_ref[:, rows], weight_ref[:half, :], (((0,), (0,)), ((), ())), preferred_element_type=F32
        )
        pre_ref[rows, :] = pre + bias_ref[...]


def dense_self(own_self, weight, bias):
    sources, own, width, side = own_self.shape
    vmem = pl.BlockSpec(memory_space=pltpu.VMEM)
    return pl.pallas_call(
        dense_self_body,
        out_shape=(
            pltpu.HBM((sources * width, own * side), BF),
            pltpu.HBM((own * side, weight.shape[1]), F32),
        ),
        in_specs=[vmem] * 3,
        out_specs=(vmem,) * 2,
        compiler_params=pltpu.CompilerParams(vmem_limit_bytes=56 * MIB),
        name="dense_self",
    )(in_vmem(own_self), in_hbm(weight), in_hbm(bias))


def dense_rest_body(
    core_ref, agg_ref, comb_self_hbm, pre_hbm, weight_hbm, cot_hbm,
    total_hbm, comb_ref, grad_ref, send_ref,
    comb_self_ref, pre_ref, weight_ref, cot_ref, sem,
):
    half, nodes = comb_ref.shape
    chunk = nodes // 2
    chunks = [pl.ds(m * chunk, chunk) for m in range(2)]
    sources = [(weight_hbm.at[pl.ds(half, half)], weight_ref)]
    for rows in chunks:
        sources.append((pre_hbm.at[rows], pre_ref.at[rows]))
        sources.append((cot_hbm.at[rows], cot_ref.at[rows]))
    sources.append((comb_self_hbm, comb_self_ref))
    loads = [pltpu.make_async_copy(a, b, sem.at[i]) for i, (a, b) in enumerate(sources)]
    for load in loads:
        load.start()
    stack_channels(agg_ref, comb_ref)
    loads[0].wait()
    stores = []
    for m, rows in enumerate(chunks):
        part = lax.dot_general(
            comb_ref[:, rows], weight_ref[...], (((0,), (0,)), ((), ())), preferred_element_type=F32
        )
        loads[1 + 2 * m].wait()
        loads[2 + 2 * m].wait()
        pre = pre_ref[rows, :] + part
        pre_ref[rows, :] = pre
        stores.append(pltpu.make_async_copy(pre_ref.at[rows], total_hbm.at[rows], sem.at[6 + m]))
        stores[m].start()
        grad_ref[rows, :] = (cot_ref[rows, :].astype(F32) * jnp.exp(jnp.minimum(pre, 0.0))).astype(BF)
    loads[5].wait()
    weight_terms(1 - core_ref[0], comb_self_ref, comb_ref, grad_ref, send_ref)
    for store in stores:
        store.wait()


def weight_terms(dest, comb_self_ref, comb_ref, grad_ref, out_ref):
    blocks, share, hid = out_ref.shape
    lhs = jnp.concatenate(
        [
            source[pl.ds(pl.multiple_of((2 * b + dest) * share, share), share), :]
            for source in (comb_self_ref, comb_ref)
            for b in range(blocks // 2)
        ],
        axis=0,
    )
    width = hid // 4
    for n in range(4):
        cols = pl.ds(n * width, width)
        total = jnp.dot(lhs, grad_ref[:, cols], preferred_element_type=F32)
        out_ref[:, :, cols] = total.reshape(blocks, share, width).astype(out_ref.dtype)


def pieces_of(half, hid):
    return (16, half // 16, hid)


def dense_rest(core, own_agg, comb_self, pre, weight, cot):
    nodes, hid = cot.shape
    half = comb_self.shape[0]
    vmem = pl.BlockSpec(memory_space=pltpu.VMEM)
    return pl.pallas_call(
        dense_rest_body,
        out_shape=(
            pltpu.HBM((nodes, hid), F32),
            pltpu.VMEM((half, nodes), BF),
            pltpu.VMEM((nodes, hid), BF),
            pltpu.VMEM(pieces_of(half, hid), BF),
        ),
        in_specs=[pl.BlockSpec(memory_space=pltpu.SMEM), vmem]
        + [pl.BlockSpec(memory_space=pl.ANY)] * 4,
        out_specs=(pl.BlockSpec(memory_space=pl.ANY),) + (vmem,) * 3,
        scratch_shapes=[
            pltpu.VMEM((half, nodes), BF),
            pltpu.VMEM((nodes, hid), F32),
            pltpu.VMEM((half, hid), BF),
            pltpu.VMEM((nodes, hid), BF),
            pltpu.SemaphoreType.DMA((8,)),
        ],
        compiler_params=pltpu.CompilerParams(vmem_limit_bytes=24 * MIB),
        name="dense_rest",
    )(core, in_vmem(own_agg), *map(in_hbm, (comb_self, pre, weight, cot)))


def dense_keep_body(core_ref, comb_self_hbm, comb_ref, grad_ref, keep_ref, comb_self_ref, sem):
    load = pltpu.make_async_copy(comb_self_hbm, comb_self_ref, sem)
    load.start()
    load.wait()
    weight_terms(core_ref[0], comb_self_ref, comb_ref, grad_ref, keep_ref)


def dense_keep(core, comb_self, comb_agg, grad):
    half, nodes = comb_self.shape
    hid = grad.shape[1]
    vmem = pl.BlockSpec(memory_space=pltpu.VMEM)
    return pl.pallas_call(
        dense_keep_body,
        out_shape=pltpu.VMEM(pieces_of(half, hid), F32),
        in_specs=[pl.BlockSpec(memory_space=pltpu.SMEM), pl.BlockSpec(memory_space=pl.ANY), vmem, vmem],
        out_specs=vmem,
        scratch_shapes=[pltpu.VMEM((half, nodes), BF), pltpu.SemaphoreType.DMA(())],
        compiler_params=pltpu.CompilerParams(vmem_limit_bytes=16 * MIB),
        name="dense_keep",
    )(core, in_hbm(comb_self), in_vmem(comb_agg), in_vmem(grad))


def sum_pieces_body(pieces_ref, sum_ref):
    sum_ref[...] = jnp.sum(pieces_ref[...].astype(F32), axis=0).astype(BF)


def sum_pieces(pieces):
    vmem = pl.BlockSpec(memory_space=pltpu.VMEM)
    return pl.pallas_call(
        sum_pieces_body,
        out_shape=pltpu.VMEM(pieces.shape[1:], BF),
        in_specs=[vmem],
        out_specs=vmem,
        compiler_params=pltpu.CompilerParams(vmem_limit_bytes=16 * MIB),
        name="sum_pieces",
    )(in_vmem(pieces))


def hidden_body(pre_ref, after_ref, hidden_ref):
    pre = pre_ref[...]
    hidden_ref[...] = jnp.where(pre > 0, pre, jnp.exp(jnp.minimum(pre, 0.0)) - 1.0).astype(BF)


def hidden_of(pre, after):
    nodes, hid = pre.shape
    rows = nodes // 8
    return pl.pallas_call(
        hidden_body,
        out_shape=jax.ShapeDtypeStruct((nodes, hid), BF),
        grid=(8,),
        in_specs=[pl.BlockSpec((rows, hid), lambda i: (i, 0)), pl.BlockSpec(memory_space=pl.ANY)],
        out_specs=pl.BlockSpec((rows, hid), lambda i: (i, 0)),
        compiler_params=pltpu.CompilerParams(vmem_limit_bytes=56 * MIB),
        name="hidden",
    )(pre, after)


def shift(value, axis, k):
    return lax.ppermute(value, axis, [(i, (i + k) % 4) for i in range(4)])


FEAT = ("x", "y", "core")


def per_device(
    features, adj_tiles, tile_rows, tile_cols, self_blocks, weight, proj_bias, cotangent
):
    feat = features[0]
    width, side = feat.shape[1:]
    nrb = self_blocks.shape[1]
    mine = gather_self(self_blocks, feat)
    feat, mine = lax.optimization_barrier((feat, mine))
    own_self = lax.all_to_all(mine, FEAT, 0, 0, tiled=True)
    agg = aggregate_tiles(tile_rows, tile_cols, feat, adj_tiles[0], nrb)
    own_agg = lax.all_to_all(agg, FEAT, 0, 0, tiled=True)
    shape = (32, nrb // 32, width, side)
    comb_self, pre = dense_self(own_self.reshape(shape), weight, proj_bias[None])
    core = lax.axis_index("core").astype(jnp.int32).reshape(1)
    pre, comb_agg, grad, send = dense_rest(
        core, own_agg.reshape(shape), comb_self, pre, weight, cotangent[0]
    )
    other = lax.ppermute(send, "core", [(0, 1), (1, 0)])
    keep = dense_keep(core, comb_self, comb_agg, grad)
    pair = (keep + other.astype(F32)).astype(BF)
    pieces = lax.all_to_all(pair, ("x", "y"), 0, 0, tiled=True)
    mine = sum_pieces(pieces)
    hidden = hidden_of(pre, mine)
    n1, n2, n3 = (shift(mine, "grp", -k).astype(F32) for k in (1, 2, 3))
    odd = lax.axis_index("grp") % 2 == 1
    total = (mine.astype(F32) + jnp.where(odd, n3, n1)) + (n2 + jnp.where(odd, n1, n3))
    return hidden[None], total


def solution(mesh):
    names = ("grp", "x", "y", "core")
    fine = Mesh(mesh.devices.reshape(4, 4, 4, 2), names)
    return jax.shard_map(
        per_device,
        mesh=fine,
        in_specs=(
            P("grp", None, FEAT, None),
            P("grp", None, None, None),
            P("grp", None),
            P("grp", None),
            P("grp", None),
            P(),
            P(),
            P("grp", FEAT, None),
        ),
        out_specs=(P("grp", FEAT, None), P(FEAT, None)),
        check_vma=False,
    )
```

```python
import functools

import jax
import jax.numpy as jnp
from jax import lax
from jax.experimental import pallas as pl
from jax.experimental.pallas import tpu as pltpu
from jax.sharding import Mesh, PartitionSpec as P

BF = jnp.bfloat16
F32 = jnp.float32
MIB = 1 << 20


def in_vmem(value):
    return pltpu.with_memory_space_constraint(value, pltpu.VMEM)


def in_hbm(value):
    return pltpu.with_memory_space_constraint(value, pltpu.HBM)


def gather_body(blocks_ref, feat_ref, out_ref, sem):
    count = out_ref.shape[0]

    def start(r, carry):
        pltpu.make_async_copy(feat_ref.at[blocks_ref[0, r]], out_ref.at[r], sem).start()
        return carry

    lax.fori_loop(0, count, start, 0, unroll=8)
    pltpu.make_async_copy(feat_ref.at[pl.ds(0, count)], out_ref, sem).wait()


def gather_self(blocks, feat):
    count = blocks.shape[1]
    return pl.pallas_call(
        gather_body,
        out_shape=jax.ShapeDtypeStruct((count,) + feat.shape[1:], feat.dtype),
        grid_spec=pltpu.PrefetchScalarGridSpec(
            num_scalar_prefetch=1,
            grid=(1,),
            in_specs=[pl.BlockSpec(memory_space=pl.ANY)],
            out_specs=pl.BlockSpec((count,) + feat.shape[1:], lambda i, b: (0, 0, 0)),
            scratch_shapes=[pltpu.SemaphoreType.DMA(())],
        ),
        compiler_params=pltpu.CompilerParams(vmem_limit_bytes=56 * MIB),
        name="gather_self",
    )(blocks, feat)


def aggregate_body(unroll, rows_ref, cols_ref, feat_ref, adj_ref, out_ref, acc_ref, part_ref):
    step = pl.program_id(0)
    tiles = adj_ref.shape[0]
    base = step * tiles

    @pl.when(step == 0)
    def _():
        acc_ref[...] = jnp.zeros_like(acc_ref)

    def multiply(k, carry):
        for u in range(unroll):
            local = k * unroll + u
            part_ref[local] = lax.dot_general(
                feat_ref[cols_ref[0, base + local]],
                adj_ref[local],
                (((1,), (1,)), ((), ())),
                preferred_element_type=F32,
            )
        return carry

    lax.fori_loop(0, tiles // unroll, multiply, 0)

    def add(k, acc):
        for u in range(unroll):
            local = k * unroll + u
            tile = base + local
            row = rows_ref[0, tile]
            same = jnp.logical_and(tile > 0, rows_ref[0, jnp.maximum(tile - 1, 0)] == row)
            keep = jnp.where(same, 1.0, 0.0).astype(F32)
            acc = part_ref[local] + acc * keep
            out_ref[row] = acc.astype(BF)
        return acc

    acc_ref[...] = lax.fori_loop(0, tiles // unroll, add, acc_ref[...])


def aggregate_tiles(rows, cols, feat, adj, nrb, steps=8, unroll=12):
    count, side, _ = adj.shape
    width = feat.shape[1]
    return pl.pallas_call(
        functools.partial(aggregate_body, unroll),
        out_shape=jax.ShapeDtypeStruct((nrb, width, side), BF),
        grid_spec=pltpu.PrefetchScalarGridSpec(
            num_scalar_prefetch=2,
            grid=(steps,),
            in_specs=[
                pl.BlockSpec(feat.shape, lambda i, a, b: (0, 0, 0), pipeline_mode=pl.Buffered(1)),
                pl.BlockSpec((count // steps, side, side), lambda i, a, b: (i, 0, 0)),
            ],
            out_specs=pl.BlockSpec((nrb, width, side), lambda i, a, b: (0, 0, 0)),
            scratch_shapes=[
                pltpu.VMEM((width, side), F32),
                pltpu.VMEM((count // steps, width, side), F32),
            ],
        ),
        compiler_params=pltpu.CompilerParams(
            vmem_limit_bytes=56 * MIB, dimension_semantics=("arbitrary",)
        ),
        cost_estimate=pl.CostEstimate(
            flops=2 * count * width * side * side,
            transcendentals=0,
            bytes_accessed=2 * (feat.size + adj.size + nrb * width * side),
        ),
        name="aggregate_tiles",
    )(rows, cols, feat, adj)


def stack_channels(own_ref, comb_ref):
    sources, own, width, side = own_ref.shape
    for r in range(own):
        comb_ref[:, pl.ds(r * side, side)] = own_ref[:, r].reshape(sources * width, side)


def dense_self_body(self_ref, weight_ref, bias_ref, comb_ref, pre_ref):
    stack_channels(self_ref, comb_ref)
    half, nodes = comb_ref.shape
    chunk = nodes // 2
    for m in range(2):
        rows = pl.ds(m * chunk, chunk)
        pre = lax.dot_general(
            comb_ref[:, rows], weight_ref[:half, :], (((0,), (0,)), ((), ())), preferred_element_type=F32
        )
        pre_ref[rows, :] = pre + bias_ref[...]


def dense_self(own_self, weight, bias):
    sources, own, width, side = own_self.shape
    vmem = pl.BlockSpec(memory_space=pltpu.VMEM)
    return pl.pallas_call(
        dense_self_body,
        out_shape=(
            pltpu.HBM((sources * width, own * side), BF),
            pltpu.HBM((own * side, weight.shape[1]), F32),
        ),
        in_specs=[vmem] * 3,
        out_specs=(vmem,) * 2,
        compiler_params=pltpu.CompilerParams(vmem_limit_bytes=56 * MIB),
        name="dense_self",
    )(in_vmem(own_self), in_hbm(weight), in_hbm(bias))


def dense_rest_body(
    core_ref, agg_ref, comb_self_hbm, pre_hbm, weight_hbm, cot_hbm,
    hidden_hbm, comb_ref, grad_ref, send_ref,
    comb_self_ref, pre_ref, weight_ref, cot_ref, hidden_ref, sem,
):
    half, nodes = comb_ref.shape
    chunk = nodes // 2
    chunks = [pl.ds(m * chunk, chunk) for m in range(2)]
    sources = [(weight_hbm.at[pl.ds(half, half)], weight_ref)]
    for rows in chunks:
        sources.append((pre_hbm.at[rows], pre_ref.at[rows]))
        sources.append((cot_hbm.at[rows], cot_ref.at[rows]))
    sources.append((comb_self_hbm, comb_self_ref))
    loads = [pltpu.make_async_copy(a, b, sem.at[i]) for i, (a, b) in enumerate(sources)]
    for load in loads:
        load.start()
    stack_channels(agg_ref, comb_ref)
    loads[0].wait()
    stores = []
    for m, rows in enumerate(chunks):
        part = lax.dot_general(
            comb_ref[:, rows], weight_ref[...], (((0,), (0,)), ((), ())), preferred_element_type=F32
        )
        loads[1 + 2 * m].wait()
        loads[2 + 2 * m].wait()
        pre = pre_ref[rows, :] + part
        decay = jnp.exp(jnp.minimum(pre, 0.0))
        hidden_ref[rows, :] = jnp.where(pre > 0, pre, decay - 1.0).astype(BF)
        grad_ref[rows, :] = (cot_ref[rows, :].astype(F32) * decay).astype(BF)
        stores.append(pltpu.make_async_copy(hidden_ref.at[rows], hidden_hbm.at[rows], sem.at[6 + m]))
        stores[m].start()
    loads[5].wait()
    weight_terms(1 - core_ref[0], comb_self_ref, comb_ref, grad_ref, send_ref)
    for store in stores:
        store.wait()


def weight_terms(dest, comb_self_ref, comb_ref, grad_ref, out_ref):
    blocks, share, hid = out_ref.shape
    lhs = jnp.concatenate(
        [
            source[pl.ds(pl.multiple_of((2 * b + dest) * share, share), share), :]
            for source in (comb_self_ref, comb_ref)
            for b in range(blocks // 2)
        ],
        axis=0,
    )
    width = hid // 4
    for n in range(4):
        cols = pl.ds(n * width, width)
        total = jnp.dot(lhs, grad_ref[:, cols], preferred_element_type=F32)
        out_ref[:, :, cols] = total.reshape(blocks, share, width).astype(out_ref.dtype)


def pieces_of(half, hid):
    return (16, half // 16, hid)


def dense_rest(core, own_agg, comb_self, pre, weight, cot):
    nodes, hid = cot.shape
    half = comb_self.shape[0]
    vmem = pl.BlockSpec(memory_space=pltpu.VMEM)
    return pl.pallas_call(
        dense_rest_body,
        out_shape=(
            pltpu.HBM((nodes, hid), BF),
            pltpu.VMEM((half, nodes), BF),
            pltpu.VMEM((nodes, hid), BF),
            pltpu.VMEM(pieces_of(half, hid), BF),
        ),
        in_specs=[pl.BlockSpec(memory_space=pltpu.SMEM), vmem]
        + [pl.BlockSpec(memory_space=pl.ANY)] * 4,
        out_specs=(pl.BlockSpec(memory_space=pl.ANY),) + (vmem,) * 3,
        scratch_shapes=[
            pltpu.VMEM((half, nodes), BF),
            pltpu.VMEM((nodes, hid), F32),
            pltpu.VMEM((half, hid), BF),
            pltpu.VMEM((nodes, hid), BF),
            pltpu.VMEM((nodes, hid), BF),
            pltpu.SemaphoreType.DMA((8,)),
        ],
        compiler_params=pltpu.CompilerParams(vmem_limit_bytes=24 * MIB),
        name="dense_rest",
    )(core, in_vmem(own_agg), *map(in_hbm, (comb_self, pre, weight, cot)))


def dense_keep_body(core_ref, comb_self_hbm, comb_ref, grad_ref, keep_ref, comb_self_ref, sem):
    load = pltpu.make_async_copy(comb_self_hbm, comb_self_ref, sem)
    load.start()
    load.wait()
    weight_terms(core_ref[0], comb_self_ref, comb_ref, grad_ref, keep_ref)


def dense_keep(core, comb_self, comb_agg, grad):
    half, nodes = comb_self.shape
    hid = grad.shape[1]
    vmem = pl.BlockSpec(memory_space=pltpu.VMEM)
    return pl.pallas_call(
        dense_keep_body,
        out_shape=pltpu.VMEM(pieces_of(half, hid), F32),
        in_specs=[pl.BlockSpec(memory_space=pltpu.SMEM), pl.BlockSpec(memory_space=pl.ANY), vmem, vmem],
        out_specs=vmem,
        scratch_shapes=[pltpu.VMEM((half, nodes), BF), pltpu.SemaphoreType.DMA(())],
        compiler_params=pltpu.CompilerParams(vmem_limit_bytes=16 * MIB),
        name="dense_keep",
    )(core, in_hbm(comb_self), in_vmem(comb_agg), in_vmem(grad))


def sum_pieces_body(pieces_ref, sum_ref):
    sum_ref[...] = jnp.sum(pieces_ref[...].astype(F32), axis=0).astype(BF)


def sum_pieces(pieces):
    vmem = pl.BlockSpec(memory_space=pltpu.VMEM)
    return pl.pallas_call(
        sum_pieces_body,
        out_shape=pltpu.VMEM(pieces.shape[1:], BF),
        in_specs=[vmem],
        out_specs=vmem,
        compiler_params=pltpu.CompilerParams(vmem_limit_bytes=16 * MIB),
        name="sum_pieces",
    )(in_vmem(pieces))


def shift(value, axis, k):
    return lax.ppermute(value, axis, [(i, (i + k) % 4) for i in range(4)])


FEAT = ("x", "y", "core")


def per_device(
    features, adj_tiles, tile_rows, tile_cols, self_blocks, weight, proj_bias, cotangent
):
    feat = features[0]
    width, side = feat.shape[1:]
    nrb = self_blocks.shape[1]
    mine = gather_self(self_blocks, feat)
    feat, mine = lax.optimization_barrier((feat, mine))
    own_self = lax.all_to_all(mine, FEAT, 0, 0, tiled=True)
    agg = aggregate_tiles(tile_rows, tile_cols, feat, adj_tiles[0], nrb)
    own_agg = lax.all_to_all(agg, FEAT, 0, 0, tiled=True)
    shape = (32, nrb // 32, width, side)
    comb_self, pre = dense_self(own_self.reshape(shape), weight, proj_bias[None])
    core = lax.axis_index("core").astype(jnp.int32).reshape(1)
    hidden, comb_agg, grad, send = dense_rest(
        core, own_agg.reshape(shape), comb_self, pre, weight, cotangent[0]
    )
    other = lax.ppermute(send, "core", [(0, 1), (1, 0)])
    keep = dense_keep(core, comb_self, comb_agg, grad)
    pair = (keep + other.astype(F32)).astype(BF)
    pieces = lax.all_to_all(pair, ("x", "y"), 0, 0, tiled=True)
    mine = sum_pieces(pieces)
    n1, n2, n3 = (shift(mine, "grp", -k).astype(F32) for k in (1, 2, 3))
    odd = lax.axis_index("grp") % 2 == 1
    total = (mine.astype(F32) + jnp.where(odd, n3, n1)) + (n2 + jnp.where(odd, n1, n3))
    return hidden[None], total


def solution(mesh):
    names = ("grp", "x", "y", "core")
    fine = Mesh(mesh.devices.reshape(4, 4, 4, 2), names)
    return jax.shard_map(
        per_device,
        mesh=fine,
        in_specs=(
            P("grp", None, FEAT, None),
            P("grp", None, None, None),
            P("grp", None),
            P("grp", None),
            P("grp", None),
            P(),
            P(),
            P("grp", FEAT, None),
        ),
        out_specs=(P("grp", FEAT, None), P(FEAT, None)),
        check_vma=False,
    )
```

```python
import functools

import jax
import jax.numpy as jnp
from jax import lax
from jax.experimental import pallas as pl
from jax.experimental.pallas import tpu as pltpu
from jax.sharding import Mesh, PartitionSpec as P

BF = jnp.bfloat16
F32 = jnp.float32
MIB = 1 << 20


def in_vmem(value):
    return pltpu.with_memory_space_constraint(value, pltpu.VMEM)


def in_hbm(value):
    return pltpu.with_memory_space_constraint(value, pltpu.HBM)


def gather_body(blocks_ref, feat_ref, out_ref, sem):
    count = out_ref.shape[0]

    def start(r, carry):
        pltpu.make_async_copy(feat_ref.at[blocks_ref[0, r]], out_ref.at[r], sem).start()
        return carry

    lax.fori_loop(0, count, start, 0, unroll=8)
    pltpu.make_async_copy(feat_ref.at[pl.ds(0, count)], out_ref, sem).wait()


def gather_self(blocks, feat):
    count = blocks.shape[1]
    return pl.pallas_call(
        gather_body,
        out_shape=jax.ShapeDtypeStruct((count,) + feat.shape[1:], feat.dtype),
        grid_spec=pltpu.PrefetchScalarGridSpec(
            num_scalar_prefetch=1,
            grid=(1,),
            in_specs=[pl.BlockSpec(memory_space=pl.ANY)],
            out_specs=pl.BlockSpec((count,) + feat.shape[1:], lambda i, b: (0, 0, 0)),
            scratch_shapes=[pltpu.SemaphoreType.DMA(())],
        ),
        compiler_params=pltpu.CompilerParams(vmem_limit_bytes=56 * MIB),
        name="gather_self",
    )(blocks, feat)


def aggregate_body(unroll, rows_ref, cols_ref, feat_ref, adj_ref, out_ref, acc_ref, part_ref):
    step = pl.program_id(0)
    tiles = adj_ref.shape[0]
    base = step * tiles

    @pl.when(step == 0)
    def _():
        acc_ref[...] = jnp.zeros_like(acc_ref)

    def multiply(k, carry):
        for u in range(unroll):
            local = k * unroll + u
            part_ref[local] = lax.dot_general(
                feat_ref[cols_ref[0, base + local]],
                adj_ref[local],
                (((1,), (1,)), ((), ())),
                preferred_element_type=F32,
            )
        return carry

    lax.fori_loop(0, tiles // unroll, multiply, 0)

    def add(k, acc):
        for u in range(unroll):
            local = k * unroll + u
            tile = base + local
            row = rows_ref[0, tile]
            same = jnp.logical_and(tile > 0, rows_ref[0, jnp.maximum(tile - 1, 0)] == row)
            keep = jnp.where(same, 1.0, 0.0).astype(F32)
            acc = part_ref[local] + acc * keep
            out_ref[row] = acc.astype(BF)
        return acc

    acc_ref[...] = lax.fori_loop(0, tiles // unroll, add, acc_ref[...])


def aggregate_tiles(rows, cols, feat, adj, nrb, steps=8, unroll=12):
    count, side, _ = adj.shape
    width = feat.shape[1]
    return pl.pallas_call(
        functools.partial(aggregate_body, unroll),
        out_shape=jax.ShapeDtypeStruct((nrb, width, side), BF),
        grid_spec=pltpu.PrefetchScalarGridSpec(
            num_scalar_prefetch=2,
            grid=(steps,),
            in_specs=[
                pl.BlockSpec(feat.shape, lambda i, a, b: (0, 0, 0), pipeline_mode=pl.Buffered(1)),
                pl.BlockSpec((count // steps, side, side), lambda i, a, b: (i, 0, 0)),
            ],
            out_specs=pl.BlockSpec((nrb, width, side), lambda i, a, b: (0, 0, 0)),
            scratch_shapes=[
                pltpu.VMEM((width, side), F32),
                pltpu.VMEM((count // steps, width, side), F32),
            ],
        ),
        compiler_params=pltpu.CompilerParams(
            vmem_limit_bytes=56 * MIB, dimension_semantics=("arbitrary",)
        ),
        cost_estimate=pl.CostEstimate(
            flops=2 * count * width * side * side,
            transcendentals=0,
            bytes_accessed=2 * (feat.size + adj.size + nrb * width * side),
        ),
        name="aggregate_tiles",
    )(rows, cols, feat, adj)


def stack_channels(own_ref, comb_ref):
    sources, own, width, side = own_ref.shape
    for r in range(own):
        comb_ref[:, pl.ds(r * side, side)] = own_ref[:, r].reshape(sources * width, side)


def dense_self_body(self_ref, weight_ref, bias_ref, comb_ref, pre_ref):
    stack_channels(self_ref, comb_ref)
    half, nodes = comb_ref.shape
    chunk = nodes // 2
    for m in range(2):
        rows = pl.ds(m * chunk, chunk)
        pre = lax.dot_general(
            comb_ref[:, rows], weight_ref[:half, :], (((0,), (0,)), ((), ())), preferred_element_type=F32
        )
        pre_ref[rows, :] = pre + bias_ref[...]


def dense_self(own_self, weight, bias):
    sources, own, width, side = own_self.shape
    vmem = pl.BlockSpec(memory_space=pltpu.VMEM)
    return pl.pallas_call(
        dense_self_body,
        out_shape=(
            pltpu.HBM((sources * width, own * side), BF),
            pltpu.HBM((own * side, weight.shape[1]), F32),
        ),
        in_specs=[vmem] * 3,
        out_specs=(vmem,) * 2,
        compiler_params=pltpu.CompilerParams(vmem_limit_bytes=56 * MIB),
        name="dense_self",
    )(in_vmem(own_self), in_hbm(weight), in_hbm(bias))


def dense_rest_body(
    place_ref, agg_ref, comb_self_hbm, pre_hbm, weight_hbm, cot_hbm,
    hidden_hbm, comb_ref, grad_ref, send_ref,
    pre_ref, weight_ref, cot_ref, hidden_ref, sem,
):
    half, nodes = comb_self_hbm.shape
    agg_rows = pl.ds(half, half)
    chunk = nodes // 2
    chunks = [pl.ds(m * chunk, chunk) for m in range(2)]
    sources = [(weight_hbm.at[agg_rows], weight_ref)]
    for rows in chunks:
        sources.append((pre_hbm.at[rows], pre_ref.at[rows]))
        sources.append((cot_hbm.at[rows], cot_ref.at[rows]))
    sources.append((comb_self_hbm, comb_ref.at[pl.ds(0, half)]))
    loads = [pltpu.make_async_copy(a, b, sem.at[i]) for i, (a, b) in enumerate(sources)]
    for load in loads:
        load.start()
    stack_channels(agg_ref, comb_ref.at[agg_rows])
    loads[0].wait()
    stores = []
    for m, rows in enumerate(chunks):
        part = lax.dot_general(
            comb_ref[agg_rows, rows], weight_ref[...], (((0,), (0,)), ((), ())), preferred_element_type=F32
        )
        loads[1 + 2 * m].wait()
        loads[2 + 2 * m].wait()
        pre = pre_ref[rows, :] + part
        decay = jnp.exp(jnp.minimum(pre, 0.0))
        hidden_ref[rows, :] = jnp.where(pre > 0, pre, decay - 1.0).astype(BF)
        grad_ref[rows, :] = (cot_ref[rows, :].astype(F32) * decay).astype(BF)
        stores.append(pltpu.make_async_copy(hidden_ref.at[rows], hidden_hbm.at[rows], sem.at[6 + m]))
        stores[m].start()
    loads[5].wait()
    weight_terms(place_ref, 1 - place_ref[2], comb_ref, grad_ref, send_ref)
    for store in stores:
        store.wait()


def weight_terms(place_ref, dest, comb_ref, grad_ref, out_ref):
    x, y = place_ref[0], place_ref[1]
    _, rows, width = out_ref.shape
    share = rows // 4

    def block(dx, dy):
        first = (8 * ((x + dx) % 4) + 2 * ((y + dy) % 4) + dest) * share
        return comb_ref[pl.ds(pl.multiple_of(first, share), share), :]

    for part in range(2):
        ahead = [(k + j, j) if part == 0 else (j, k + j) for k in range(4) for j in range(4)]
        lhs = jnp.concatenate([block(dx, dy) for dx, dy in ahead], axis=0)
        total = jnp.dot(lhs, grad_ref[:, pl.ds(part * width, width)], preferred_element_type=F32)
        out_ref[pl.ds(4 * part, 4)] = total.reshape(4, rows, width).astype(out_ref.dtype)


def pieces_of(half, hid):
    return (8, half // 4, hid // 2)


def dense_rest(place, own_agg, comb_self, pre, weight, cot):
    nodes, hid = cot.shape
    half = comb_self.shape[0]
    vmem = pl.BlockSpec(memory_space=pltpu.VMEM)
    return pl.pallas_call(
        dense_rest_body,
        out_shape=(
            pltpu.HBM((nodes, hid), BF),
            pltpu.VMEM((2 * half, nodes), BF),
            pltpu.VMEM((nodes, hid), BF),
            pltpu.VMEM(pieces_of(half, hid), BF),
        ),
        in_specs=[pl.BlockSpec(memory_space=pltpu.SMEM), vmem]
        + [pl.BlockSpec(memory_space=pl.ANY)] * 4,
        out_specs=(pl.BlockSpec(memory_space=pl.ANY),) + (vmem,) * 3,
        scratch_shapes=[
            pltpu.VMEM((nodes, hid), F32),
            pltpu.VMEM((half, hid), BF),
            pltpu.VMEM((nodes, hid), BF),
            pltpu.VMEM((nodes, hid), BF),
            pltpu.SemaphoreType.DMA((8,)),
        ],
        compiler_params=pltpu.CompilerParams(vmem_limit_bytes=24 * MIB),
        name="dense_rest",
    )(place, in_vmem(own_agg), *map(in_hbm, (comb_self, pre, weight, cot)))


def dense_keep_body(place_ref, comb_ref, grad_ref, keep_ref):
    weight_terms(place_ref, place_ref[2], comb_ref, grad_ref, keep_ref)


def dense_keep(place, comb, grad):
    channels = comb.shape[0]
    vmem = pl.BlockSpec(memory_space=pltpu.VMEM)
    return pl.pallas_call(
        dense_keep_body,
        out_shape=pltpu.VMEM(pieces_of(channels // 2, grad.shape[1]), F32),
        in_specs=[pl.BlockSpec(memory_space=pltpu.SMEM), vmem, vmem],
        out_specs=vmem,
        compiler_params=pltpu.CompilerParams(vmem_limit_bytes=16 * MIB),
        name="dense_keep",
    )(place, in_vmem(comb), in_vmem(grad))


def shift(value, axis, k):
    return lax.ppermute(value, axis, [(i, (i + k) % 4) for i in range(4)])


def shift_diagonal(value, k):
    pairs = [(4 * x + y, 4 * ((x + k) % 4) + (y + k) % 4) for x in range(4) for y in range(4)]
    return lax.ppermute(value, ("x", "y"), pairs)


FEAT = ("x", "y", "core")


def per_device(
    features, adj_tiles, tile_rows, tile_cols, self_blocks, weight, proj_bias, cotangent
):
    feat = features[0]
    width, side = feat.shape[1:]
    nrb = self_blocks.shape[1]
    mine = gather_self(self_blocks, feat)
    feat, mine = lax.optimization_barrier((feat, mine))
    own_self = lax.all_to_all(mine, FEAT, 0, 0, tiled=True)
    agg = aggregate_tiles(tile_rows, tile_cols, feat, adj_tiles[0], nrb)
    own_agg = lax.all_to_all(agg, FEAT, 0, 0, tiled=True)
    shape = (32, nrb // 32, width, side)
    comb_self, pre = dense_self(own_self.reshape(shape), weight, proj_bias[None])
    place = jnp.stack([lax.axis_index(a) for a in FEAT]).astype(jnp.int32)
    hidden, comb, grad, send = dense_rest(
        place, own_agg.reshape(shape), comb_self, pre, weight, cotangent[0]
    )
    other = lax.ppermute(send, "core", [(0, 1), (1, 0)])
    pair = dense_keep(place, comb, grad) + other.astype(F32)
    share, width = weight.shape[0] // 32, weight.shape[1] // 2
    moved = [
        [shift(pair[4 * part + k].astype(BF), axis, k).astype(F32) for k in (1, 2, 3)]
        for part, axis in enumerate(("x", "y"))
    ]
    once = [(pair[4 * part] + sum(moved[part])).reshape(4, share, width) for part in range(2)]
    once = jnp.concatenate(once, axis=2)
    mine = once[0] + sum(shift_diagonal(once[j].astype(BF), j).astype(F32) for j in (1, 2, 3))
    mine = mine.astype(BF)
    n1, n2, n3 = (shift(mine, "grp", -k).astype(F32) for k in (1, 2, 3))
    odd = lax.axis_index("grp") % 2 == 1
    total = (mine.astype(F32) + jnp.where(odd, n3, n1)) + (n2 + jnp.where(odd, n1, n3))
    return hidden[None], total


def solution(mesh):
    names = ("grp", "x", "y", "core")
    fine = Mesh(mesh.devices.reshape(4, 4, 4, 2), names)
    return jax.shard_map(
        per_device,
        mesh=fine,
        in_specs=(
            P("grp", None, FEAT, None),
            P("grp", None, None, None),
            P("grp", None),
            P("grp", None),
            P("grp", None),
            P(),
            P(),
            P("grp", FEAT, None),
        ),
        out_specs=(P("grp", FEAT, None), P(FEAT, None)),
        check_vma=False,
    )
```

```python
import functools

import jax
import jax.numpy as jnp
from jax import lax
from jax.experimental import pallas as pl
from jax.experimental.pallas import tpu as pltpu
from jax.sharding import Mesh, PartitionSpec as P

BF = jnp.bfloat16
F32 = jnp.float32
MIB = 1 << 20


def in_vmem(value):
    return pltpu.with_memory_space_constraint(value, pltpu.VMEM)


def in_hbm(value):
    return pltpu.with_memory_space_constraint(value, pltpu.HBM)


def gather_body(blocks_ref, feat_ref, out_hbm, rows_ref, in_sem, out_sem):
    count = rows_ref.shape[0]
    part = count // 4

    def quarter(q):
        def start(r, carry):
            row = q * part + r
            pltpu.make_async_copy(feat_ref.at[blocks_ref[0, row]], rows_ref.at[row], in_sem.at[q]).start()
            return carry

        lax.fori_loop(0, part, start, 0, unroll=16)

    def store(q):
        rows = pl.ds(q * part, part)
        pltpu.make_async_copy(feat_ref.at[pl.ds(0, part)], rows_ref.at[rows], in_sem.at[q]).wait()
        copy = pltpu.make_async_copy(rows_ref.at[rows], out_hbm.at[rows], out_sem.at[q])
        copy.start()
        return copy

    quarter(0)
    quarter(1)
    stores = [store(0)]
    quarter(2)
    stores.append(store(1))
    quarter(3)
    stores += [store(2), store(3)]
    for copy in stores:
        copy.wait()


def gather_self(blocks, feat):
    shape = (blocks.shape[1],) + feat.shape[1:]
    return pl.pallas_call(
        gather_body,
        out_shape=jax.ShapeDtypeStruct(shape, feat.dtype),
        grid_spec=pltpu.PrefetchScalarGridSpec(
            num_scalar_prefetch=1,
            grid=(1,),
            in_specs=[pl.BlockSpec(memory_space=pl.ANY)],
            out_specs=pl.BlockSpec(memory_space=pl.ANY),
            scratch_shapes=[
                pltpu.VMEM(shape, feat.dtype),
                pltpu.SemaphoreType.DMA((4,)),
                pltpu.SemaphoreType.DMA((4,)),
            ],
        ),
        compiler_params=pltpu.CompilerParams(vmem_limit_bytes=56 * MIB),
        name="gather_self",
    )(blocks, feat)


def aggregate_body(unroll, rows_ref, cols_ref, feat_ref, adj_ref, out_ref, acc_ref, part_ref):
    step = pl.program_id(0)
    tiles = adj_ref.shape[0]
    base = step * tiles

    @pl.when(step == 0)
    def _():
        acc_ref[...] = jnp.zeros_like(acc_ref)

    def multiply(k, carry):
        for u in range(unroll):
            local = k * unroll + u
            part_ref[local] = lax.dot_general(
                feat_ref[cols_ref[0, base + local]],
                adj_ref[local],
                (((1,), (1,)), ((), ())),
                preferred_element_type=F32,
            )
        return carry

    lax.fori_loop(0, tiles // unroll, multiply, 0)

    def add(k, acc):
        for u in range(unroll):
            local = k * unroll + u
            tile = base + local
            row = rows_ref[0, tile]
            same = jnp.logical_and(tile > 0, rows_ref[0, jnp.maximum(tile - 1, 0)] == row)
            keep = jnp.where(same, 1.0, 0.0).astype(F32)
            acc = part_ref[local] + acc * keep
            out_ref[row] = acc.astype(BF)
        return acc

    acc_ref[...] = lax.fori_loop(0, tiles // unroll, add, acc_ref[...])


def aggregate_tiles(rows, cols, feat, adj, nrb, steps=8, unroll=12):
    count, side, _ = adj.shape
    width = feat.shape[1]
    return pl.pallas_call(
        functools.partial(aggregate_body, unroll),
        out_shape=jax.ShapeDtypeStruct((nrb, width, side), BF),
        grid_spec=pltpu.PrefetchScalarGridSpec(
            num_scalar_prefetch=2,
            grid=(steps,),
            in_specs=[
                pl.BlockSpec(feat.shape, lambda i, a, b: (0, 0, 0), pipeline_mode=pl.Buffered(1)),
                pl.BlockSpec((count // steps, side, side), lambda i, a, b: (i, 0, 0)),
            ],
            out_specs=pl.BlockSpec((nrb, width, side), lambda i, a, b: (0, 0, 0)),
            scratch_shapes=[
                pltpu.VMEM((width, side), F32),
                pltpu.VMEM((count // steps, width, side), F32),
            ],
        ),
        compiler_params=pltpu.CompilerParams(
            vmem_limit_bytes=56 * MIB, dimension_semantics=("arbitrary",)
        ),
        cost_estimate=pl.CostEstimate(
            flops=2 * count * width * side * side,
            transcendentals=0,
            bytes_accessed=2 * (feat.size + adj.size + nrb * width * side),
        ),
        name="aggregate_tiles",
    )(rows, cols, feat, adj)


def stack_channels(own_ref, comb_ref):
    sources, own, width, side = own_ref.shape
    for r in range(own):
        comb_ref[:, pl.ds(r * side, side)] = own_ref[:, r].reshape(sources * width, side)


def dense_self_body(self_ref, weight_ref, bias_ref, comb_ref, pre_ref):
    stack_channels(self_ref, comb_ref)
    half, nodes = comb_ref.shape
    chunk = nodes // 2
    for m in range(2):
        rows = pl.ds(m * chunk, chunk)
        pre = lax.dot_general(
            comb_ref[:, rows], weight_ref[:half, :], (((0,), (0,)), ((), ())), preferred_element_type=F32
        )
        pre_ref[rows, :] = pre + bias_ref[...]


def dense_self(own_self, weight, bias):
    sources, own, width, side = own_self.shape
    vmem = pl.BlockSpec(memory_space=pltpu.VMEM)
    return pl.pallas_call(
        dense_self_body,
        out_shape=(
            pltpu.HBM((sources * width, own * side), BF),
            pltpu.HBM((own * side, weight.shape[1]), F32),
        ),
        in_specs=[vmem] * 3,
        out_specs=(vmem,) * 2,
        compiler_params=pltpu.CompilerParams(vmem_limit_bytes=56 * MIB),
        name="dense_self",
    )(in_vmem(own_self), in_hbm(weight), in_hbm(bias))


def dense_rest_body(
    core_ref, agg_ref, comb_self_hbm, pre_hbm, weight_hbm, cot_hbm,
    hidden_hbm, comb_ref, grad_ref, send_ref,
    comb_self_ref, pre_ref, weight_ref, cot_ref, hidden_ref, sem,
):
    half, nodes = comb_ref.shape
    chunk = nodes // 2
    chunks = [pl.ds(m * chunk, chunk) for m in range(2)]
    sources = [(weight_hbm.at[pl.ds(half, half)], weight_ref)]
    for rows in chunks:
        sources.append((pre_hbm.at[rows], pre_ref.at[rows]))
        sources.append((cot_hbm.at[rows], cot_ref.at[rows]))
    sources.append((comb_self_hbm, comb_self_ref))
    loads = [pltpu.make_async_copy(a, b, sem.at[i]) for i, (a, b) in enumerate(sources)]
    for load in loads:
        load.start()
    stack_channels(agg_ref, comb_ref)
    loads[0].wait()
    stores = []
    for m, rows in enumerate(chunks):
        part = lax.dot_general(
            comb_ref[:, rows], weight_ref[...], (((0,), (0,)), ((), ())), preferred_element_type=F32
        )
        loads[1 + 2 * m].wait()
        loads[2 + 2 * m].wait()
        pre = pre_ref[rows, :] + part
        decay = jnp.exp(jnp.minimum(pre, 0.0))
        hidden_ref[rows, :] = jnp.where(pre > 0, pre, decay - 1.0).astype(BF)
        grad_ref[rows, :] = (cot_ref[rows, :].astype(F32) * decay).astype(BF)
        stores.append(pltpu.make_async_copy(hidden_ref.at[rows], hidden_hbm.at[rows], sem.at[6 + m]))
        stores[m].start()
    loads[5].wait()
    weight_terms(1 - core_ref[0], comb_self_ref, comb_ref, grad_ref, send_ref)
    for store in stores:
        store.wait()


def weight_terms(dest, comb_self_ref, comb_ref, grad_ref, out_ref):
    blocks, share, hid = out_ref.shape
    lhs = jnp.concatenate(
        [
            source[pl.ds(pl.multiple_of((2 * b + dest) * share, share), share), :]
            for source in (comb_self_ref, comb_ref)
            for b in range(blocks // 2)
        ],
        axis=0,
    )
    width = hid // 4
    for n in range(4):
        cols = pl.ds(n * width, width)
        total = jnp.dot(lhs, grad_ref[:, cols], preferred_element_type=F32)
        out_ref[:, :, cols] = total.reshape(blocks, share, width).astype(out_ref.dtype)


def pieces_of(half, hid):
    return (16, half // 16, hid)


def dense_rest(core, own_agg, comb_self, pre, weight, cot):
    nodes, hid = cot.shape
    half = comb_self.shape[0]
    vmem = pl.BlockSpec(memory_space=pltpu.VMEM)
    return pl.pallas_call(
        dense_rest_body,
        out_shape=(
            pltpu.HBM((nodes, hid), BF),
            pltpu.VMEM((half, nodes), BF),
            pltpu.VMEM((nodes, hid), BF),
            pltpu.VMEM(pieces_of(half, hid), BF),
        ),
        in_specs=[pl.BlockSpec(memory_space=pltpu.SMEM), vmem]
        + [pl.BlockSpec(memory_space=pl.ANY)] * 4,
        out_specs=(pl.BlockSpec(memory_space=pl.ANY),) + (vmem,) * 3,
        scratch_shapes=[
            pltpu.VMEM((half, nodes), BF),
            pltpu.VMEM((nodes, hid), F32),
            pltpu.VMEM((half, hid), BF),
            pltpu.VMEM((nodes, hid), BF),
            pltpu.VMEM((nodes, hid), BF),
            pltpu.SemaphoreType.DMA((8,)),
        ],
        compiler_params=pltpu.CompilerParams(vmem_limit_bytes=24 * MIB),
        name="dense_rest",
    )(core, in_vmem(own_agg), *map(in_hbm, (comb_self, pre, weight, cot)))


def dense_keep_body(core_ref, comb_self_hbm, comb_ref, grad_ref, keep_ref, comb_self_ref, sem):
    load = pltpu.make_async_copy(comb_self_hbm, comb_self_ref, sem)
    load.start()
    load.wait()
    weight_terms(core_ref[0], comb_self_ref, comb_ref, grad_ref, keep_ref)


def dense_keep(core, comb_self, comb_agg, grad):
    half, nodes = comb_self.shape
    hid = grad.shape[1]
    vmem = pl.BlockSpec(memory_space=pltpu.VMEM)
    return pl.pallas_call(
        dense_keep_body,
        out_shape=pltpu.VMEM(pieces_of(half, hid), F32),
        in_specs=[pl.BlockSpec(memory_space=pltpu.SMEM), pl.BlockSpec(memory_space=pl.ANY), vmem, vmem],
        out_specs=vmem,
        scratch_shapes=[pltpu.VMEM((half, nodes), BF), pltpu.SemaphoreType.DMA(())],
        compiler_params=pltpu.CompilerParams(vmem_limit_bytes=16 * MIB),
        name="dense_keep",
    )(core, in_hbm(comb_self), in_vmem(comb_agg), in_vmem(grad))


def sum_pieces_body(pieces_ref, sum_ref):
    sum_ref[...] = jnp.sum(pieces_ref[...].astype(F32), axis=0).astype(BF)


def sum_pieces(pieces):
    vmem = pl.BlockSpec(memory_space=pltpu.VMEM)
    return pl.pallas_call(
        sum_pieces_body,
        out_shape=pltpu.VMEM(pieces.shape[1:], BF),
        in_specs=[vmem],
        out_specs=vmem,
        compiler_params=pltpu.CompilerParams(vmem_limit_bytes=16 * MIB),
        name="sum_pieces",
    )(in_vmem(pieces))


def shift(value, axis, k):
    return lax.ppermute(value, axis, [(i, (i + k) % 4) for i in range(4)])


FEAT = ("x", "y", "core")


def per_device(
    features, adj_tiles, tile_rows, tile_cols, self_blocks, weight, proj_bias, cotangent
):
    feat = features[0]
    width, side = feat.shape[1:]
    nrb = self_blocks.shape[1]
    mine = gather_self(self_blocks, feat)
    feat, mine = lax.optimization_barrier((feat, mine))
    own_self = lax.all_to_all(mine, FEAT, 0, 0, tiled=True)
    agg = aggregate_tiles(tile_rows, tile_cols, feat, adj_tiles[0], nrb)
    own_agg = lax.all_to_all(agg, FEAT, 0, 0, tiled=True)
    shape = (32, nrb // 32, width, side)
    comb_self, pre = dense_self(own_self.reshape(shape), weight, proj_bias[None])
    core = lax.axis_index("core").astype(jnp.int32).reshape(1)
    hidden, comb_agg, grad, send = dense_rest(
        core, own_agg.reshape(shape), comb_self, pre, weight, cotangent[0]
    )
    other = lax.ppermute(send, "core", [(0, 1), (1, 0)])
    keep = dense_keep(core, comb_self, comb_agg, grad)
    pair = (keep + other.astype(F32)).astype(BF)
    pieces = lax.all_to_all(pair, ("x", "y"), 0, 0, tiled=True)
    mine = sum_pieces(pieces)
    n1, n2, n3 = (shift(mine, "grp", -k).astype(F32) for k in (1, 2, 3))
    odd = lax.axis_index("grp") % 2 == 1
    total = (mine.astype(F32) + jnp.where(odd, n3, n1)) + (n2 + jnp.where(odd, n1, n3))
    return hidden[None], total


def solution(mesh):
    names = ("grp", "x", "y", "core")
    fine = Mesh(mesh.devices.reshape(4, 4, 4, 2), names)
    return jax.shard_map(
        per_device,
        mesh=fine,
        in_specs=(
            P("grp", None, FEAT, None),
            P("grp", None, None, None),
            P("grp", None),
            P("grp", None),
            P("grp", None),
            P(),
            P(),
            P("grp", FEAT, None),
        ),
        out_specs=(P("grp", FEAT, None), P(FEAT, None)),
        check_vma=False,
    )
```

```python
import functools

import jax
import jax.numpy as jnp
from jax import lax
from jax.experimental import pallas as pl
from jax.experimental.pallas import tpu as pltpu
from jax.sharding import Mesh, PartitionSpec as P

BF = jnp.bfloat16
F32 = jnp.float32
MIB = 1 << 20


def in_vmem(value):
    return pltpu.with_memory_space_constraint(value, pltpu.VMEM)


def in_hbm(value):
    return pltpu.with_memory_space_constraint(value, pltpu.HBM)


def gather_body(blocks_ref, feat_ref, out_ref, sem):
    count = out_ref.shape[0]

    def start(r, carry):
        pltpu.make_async_copy(feat_ref.at[blocks_ref[0, r]], out_ref.at[r], sem).start()
        return carry

    lax.fori_loop(0, count, start, 0, unroll=8)
    pltpu.make_async_copy(feat_ref.at[pl.ds(0, count)], out_ref, sem).wait()


def gather_self(blocks, feat):
    count = blocks.shape[1]
    return pl.pallas_call(
        gather_body,
        out_shape=jax.ShapeDtypeStruct((count,) + feat.shape[1:], feat.dtype),
        grid_spec=pltpu.PrefetchScalarGridSpec(
            num_scalar_prefetch=1,
            grid=(1,),
            in_specs=[pl.BlockSpec(memory_space=pl.ANY)],
            out_specs=pl.BlockSpec((count,) + feat.shape[1:], lambda i, b: (0, 0, 0)),
            scratch_shapes=[pltpu.SemaphoreType.DMA(())],
        ),
        compiler_params=pltpu.CompilerParams(vmem_limit_bytes=56 * MIB),
        name="gather_self",
    )(blocks, feat)


def aggregate_body(unroll, rows_ref, cols_ref, feat_ref, adj_ref, out_ref, acc_ref, part_ref):
    step = pl.program_id(0)
    tiles = adj_ref.shape[0]
    base = step * tiles

    @pl.when(step == 0)
    def _():
        acc_ref[...] = jnp.zeros_like(acc_ref)

    def multiply(k, carry):
        for u in range(unroll):
            local = k * unroll + u
            part_ref[local] = lax.dot_general(
                feat_ref[cols_ref[0, base + local]],
                adj_ref[local],
                (((1,), (1,)), ((), ())),
                preferred_element_type=F32,
            )
        return carry

    lax.fori_loop(0, tiles // unroll, multiply, 0)

    def add(k, acc):
        for u in range(unroll):
            local = k * unroll + u
            tile = base + local
            row = rows_ref[0, tile]
            same = jnp.logical_and(tile > 0, rows_ref[0, jnp.maximum(tile - 1, 0)] == row)
            keep = jnp.where(same, 1.0, 0.0).astype(F32)
            acc = part_ref[local] + acc * keep
            out_ref[row] = acc.astype(BF)
        return acc

    acc_ref[...] = lax.fori_loop(0, tiles // unroll, add, acc_ref[...])


def aggregate_tiles(rows, cols, feat, adj, nrb, steps=8, unroll=12):
    count, side, _ = adj.shape
    width = feat.shape[1]
    return pl.pallas_call(
        functools.partial(aggregate_body, unroll),
        out_shape=jax.ShapeDtypeStruct((nrb, width, side), BF),
        grid_spec=pltpu.PrefetchScalarGridSpec(
            num_scalar_prefetch=2,
            grid=(steps,),
            in_specs=[
                pl.BlockSpec(feat.shape, lambda i, a, b: (0, 0, 0), pipeline_mode=pl.Buffered(1)),
                pl.BlockSpec((count // steps, side, side), lambda i, a, b: (i, 0, 0)),
            ],
            out_specs=pl.BlockSpec((nrb, width, side), lambda i, a, b: (0, 0, 0)),
            scratch_shapes=[
                pltpu.VMEM((width, side), F32),
                pltpu.VMEM((count // steps, width, side), F32),
            ],
        ),
        compiler_params=pltpu.CompilerParams(
            vmem_limit_bytes=56 * MIB, dimension_semantics=("arbitrary",)
        ),
        cost_estimate=pl.CostEstimate(
            flops=2 * count * width * side * side,
            transcendentals=0,
            bytes_accessed=2 * (feat.size + adj.size + nrb * width * side),
        ),
        name="aggregate_tiles",
    )(rows, cols, feat, adj)


def stack_channels(own_ref, comb_ref):
    sources, own, width, side = own_ref.shape
    for r in range(own):
        comb_ref[:, pl.ds(r * side, side)] = own_ref[:, r].reshape(sources * width, side)


def dense_self_body(self_ref, weight_ref, bias_ref, comb_ref, pre_ref):
    stack_channels(self_ref, comb_ref)
    half, nodes = comb_ref.shape
    chunk = nodes // 2
    for m in range(2):
        rows = pl.ds(m * chunk, chunk)
        pre = lax.dot_general(
            comb_ref[:, rows], weight_ref[:half, :], (((0,), (0,)), ((), ())), preferred_element_type=F32
        )
        pre_ref[rows, :] = pre + bias_ref[...]


def dense_self(own_self, weight, bias):
    sources, own, width, side = own_self.shape
    vmem = pl.BlockSpec(memory_space=pltpu.VMEM)
    return pl.pallas_call(
        dense_self_body,
        out_shape=(
            pltpu.HBM((sources * width, own * side), BF),
            pltpu.HBM((own * side, weight.shape[1]), F32),
        ),
        in_specs=[vmem] * 3,
        out_specs=(vmem,) * 2,
        compiler_params=pltpu.CompilerParams(vmem_limit_bytes=56 * MIB),
        name="dense_self",
    )(in_vmem(own_self), in_hbm(weight), in_hbm(bias))


def dense_rest_body(
    core_ref, agg_ref, comb_self_hbm, pre_hbm, weight_hbm, cot_hbm,
    hidden_hbm, comb_ref, grad_ref, send_ref,
    comb_self_ref, pre_ref, weight_ref, cot_ref, hidden_ref, sem,
):
    half, nodes = comb_ref.shape
    sources = [
        (weight_hbm.at[pl.ds(half, half)], weight_ref),
        (pre_hbm, pre_ref),
        (cot_hbm, cot_ref),
        (comb_self_hbm, comb_self_ref),
    ]
    loads = [pltpu.make_async_copy(a, b, sem.at[i]) for i, (a, b) in enumerate(sources)]
    for load in loads:
        load.start()
    stack_channels(agg_ref, comb_ref)
    loads[0].wait()
    part = lax.dot_general(
        comb_ref[...], weight_ref[...], (((0,), (0,)), ((), ())), preferred_element_type=F32
    )
    loads[1].wait()
    loads[2].wait()
    pre = pre_ref[...] + part
    decay = jnp.exp(jnp.minimum(pre, 0.0))
    hidden_ref[...] = jnp.where(pre > 0, pre, decay - 1.0).astype(BF)
    grad_ref[...] = (cot_ref[...].astype(F32) * decay).astype(BF)
    store = pltpu.make_async_copy(hidden_ref, hidden_hbm, sem.at[4])
    store.start()
    loads[3].wait()
    weight_terms(1 - core_ref[0], comb_self_ref, comb_ref, grad_ref, send_ref)
    store.wait()


def weight_terms(dest, comb_self_ref, comb_ref, grad_ref, out_ref):
    blocks, share, hid = out_ref.shape
    lhs = jnp.concatenate(
        [
            source[pl.ds(pl.multiple_of((2 * b + dest) * share, share), share), :]
            for source in (comb_self_ref, comb_ref)
            for b in range(blocks // 2)
        ],
        axis=0,
    )
    width = hid // 4
    for n in range(4):
        cols = pl.ds(n * width, width)
        total = jnp.dot(lhs, grad_ref[:, cols], preferred_element_type=F32)
        out_ref[:, :, cols] = total.reshape(blocks, share, width).astype(out_ref.dtype)


def pieces_of(half, hid):
    return (16, half // 16, hid)


def dense_rest(core, own_agg, comb_self, pre, weight, cot):
    nodes, hid = cot.shape
    half = comb_self.shape[0]
    vmem = pl.BlockSpec(memory_space=pltpu.VMEM)
    return pl.pallas_call(
        dense_rest_body,
        out_shape=(
            pltpu.HBM((nodes, hid), BF),
            pltpu.VMEM((half, nodes), BF),
            pltpu.VMEM((nodes, hid), BF),
            pltpu.VMEM(pieces_of(half, hid), BF),
        ),
        in_specs=[pl.BlockSpec(memory_space=pltpu.SMEM), vmem]
        + [pl.BlockSpec(memory_space=pl.ANY)] * 4,
        out_specs=(pl.BlockSpec(memory_space=pl.ANY),) + (vmem,) * 3,
        scratch_shapes=[
            pltpu.VMEM((half, nodes), BF),
            pltpu.VMEM((nodes, hid), F32),
            pltpu.VMEM((half, hid), BF),
            pltpu.VMEM((nodes, hid), BF),
            pltpu.VMEM((nodes, hid), BF),
            pltpu.SemaphoreType.DMA((5,)),
        ],
        compiler_params=pltpu.CompilerParams(vmem_limit_bytes=24 * MIB),
        name="dense_rest",
    )(core, in_vmem(own_agg), *map(in_hbm, (comb_self, pre, weight, cot)))


def dense_keep_body(core_ref, comb_self_hbm, comb_ref, grad_ref, keep_ref, comb_self_ref, sem):
    load = pltpu.make_async_copy(comb_self_hbm, comb_self_ref, sem)
    load.start()
    load.wait()
    weight_terms(core_ref[0], comb_self_ref, comb_ref, grad_ref, keep_ref)


def dense_keep(core, comb_self, comb_agg, grad):
    half, nodes = comb_self.shape
    hid = grad.shape[1]
    vmem = pl.BlockSpec(memory_space=pltpu.VMEM)
    return pl.pallas_call(
        dense_keep_body,
        out_shape=pltpu.VMEM(pieces_of(half, hid), F32),
        in_specs=[pl.BlockSpec(memory_space=pltpu.SMEM), pl.BlockSpec(memory_space=pl.ANY), vmem, vmem],
        out_specs=vmem,
        scratch_shapes=[pltpu.VMEM((half, nodes), BF), pltpu.SemaphoreType.DMA(())],
        compiler_params=pltpu.CompilerParams(vmem_limit_bytes=16 * MIB),
        name="dense_keep",
    )(core, in_hbm(comb_self), in_vmem(comb_agg), in_vmem(grad))


def sum_pieces_body(pieces_ref, sum_ref):
    sum_ref[...] = jnp.sum(pieces_ref[...].astype(F32), axis=0).astype(BF)


def sum_pieces(pieces):
    vmem = pl.BlockSpec(memory_space=pltpu.VMEM)
    return pl.pallas_call(
        sum_pieces_body,
        out_shape=pltpu.VMEM(pieces.shape[1:], BF),
        in_specs=[vmem],
        out_specs=vmem,
        compiler_params=pltpu.CompilerParams(vmem_limit_bytes=16 * MIB),
        name="sum_pieces",
    )(in_vmem(pieces))


def shift(value, axis, k):
    return lax.ppermute(value, axis, [(i, (i + k) % 4) for i in range(4)])


FEAT = ("x", "y", "core")


def per_device(
    features, adj_tiles, tile_rows, tile_cols, self_blocks, weight, proj_bias, cotangent
):
    feat = features[0]
    width, side = feat.shape[1:]
    nrb = self_blocks.shape[1]
    mine = gather_self(self_blocks, feat)
    feat, mine = lax.optimization_barrier((feat, mine))
    own_self = lax.all_to_all(mine, FEAT, 0, 0, tiled=True)
    agg = aggregate_tiles(tile_rows, tile_cols, feat, adj_tiles[0], nrb)
    own_agg = lax.all_to_all(agg, FEAT, 0, 0, tiled=True)
    shape = (32, nrb // 32, width, side)
    comb_self, pre = dense_self(own_self.reshape(shape), weight, proj_bias[None])
    core = lax.axis_index("core").astype(jnp.int32).reshape(1)
    hidden, comb_agg, grad, send = dense_rest(
        core, own_agg.reshape(shape), comb_self, pre, weight, cotangent[0]
    )
    other = lax.ppermute(send, "core", [(0, 1), (1, 0)])
    keep = dense_keep(core, comb_self, comb_agg, grad)
    pair = (keep + other.astype(F32)).astype(BF)
    pieces = lax.all_to_all(pair, ("x", "y"), 0, 0, tiled=True)
    mine = sum_pieces(pieces)
    n1, n2, n3 = (shift(mine, "grp", -k).astype(F32) for k in (1, 2, 3))
    odd = lax.axis_index("grp") % 2 == 1
    total = (mine.astype(F32) + jnp.where(odd, n3, n1)) + (n2 + jnp.where(odd, n1, n3))
    return hidden[None], total


def solution(mesh):
    names = ("grp", "x", "y", "core")
    fine = Mesh(mesh.devices.reshape(4, 4, 4, 2), names)
    return jax.shard_map(
        per_device,
        mesh=fine,
        in_specs=(
            P("grp", None, FEAT, None),
            P("grp", None, None, None),
            P("grp", None),
            P("grp", None),
            P("grp", None),
            P(),
            P(),
            P("grp", FEAT, None),
        ),
        out_specs=(P("grp", FEAT, None), P(FEAT, None)),
        check_vma=False,
    )
```

```python
import functools

import jax
import jax.numpy as jnp
from jax import lax
from jax.experimental import pallas as pl
from jax.experimental.pallas import tpu as pltpu
from jax.sharding import Mesh, PartitionSpec as P

BF = jnp.bfloat16
F32 = jnp.float32
MIB = 1 << 20


def in_vmem(value):
    return pltpu.with_memory_space_constraint(value, pltpu.VMEM)


def in_hbm(value):
    return pltpu.with_memory_space_constraint(value, pltpu.HBM)


def gather_body(blocks_ref, feat_ref, out_ref, sem):
    count = out_ref.shape[0]

    def start(r, carry):
        pltpu.make_async_copy(feat_ref.at[blocks_ref[0, r]], out_ref.at[r], sem).start()
        return carry

    lax.fori_loop(0, count, start, 0, unroll=8)
    pltpu.make_async_copy(feat_ref.at[pl.ds(0, count)], out_ref, sem).wait()


def gather_self(blocks, feat):
    count = blocks.shape[1]
    return pl.pallas_call(
        gather_body,
        out_shape=jax.ShapeDtypeStruct((count,) + feat.shape[1:], feat.dtype),
        grid_spec=pltpu.PrefetchScalarGridSpec(
            num_scalar_prefetch=1,
            grid=(1,),
            in_specs=[pl.BlockSpec(memory_space=pl.ANY)],
            out_specs=pl.BlockSpec((count,) + feat.shape[1:], lambda i, b: (0, 0, 0)),
            scratch_shapes=[pltpu.SemaphoreType.DMA(())],
        ),
        compiler_params=pltpu.CompilerParams(vmem_limit_bytes=56 * MIB),
        name="gather_self",
    )(blocks, feat)


def aggregate_body(unroll, rows_ref, cols_ref, feat_ref, adj_ref, out_ref, acc_ref, part_ref):
    step = pl.program_id(0)
    tiles = adj_ref.shape[0]
    base = step * tiles

    @pl.when(step == 0)
    def _():
        acc_ref[...] = jnp.zeros_like(acc_ref)

    def multiply(k, carry):
        for u in range(unroll):
            local = k * unroll + u
            part_ref[local] = lax.dot_general(
                feat_ref[cols_ref[0, base + local]],
                adj_ref[local],
                (((1,), (1,)), ((), ())),
                preferred_element_type=F32,
            )
        return carry

    lax.fori_loop(0, tiles // unroll, multiply, 0)

    def add(k, acc):
        for u in range(unroll):
            local = k * unroll + u
            tile = base + local
            row = rows_ref[0, tile]
            same = jnp.logical_and(tile > 0, rows_ref[0, jnp.maximum(tile - 1, 0)] == row)
            keep = jnp.where(same, 1.0, 0.0).astype(F32)
            acc = part_ref[local] + acc * keep
            out_ref[row] = acc.astype(BF)
        return acc

    acc_ref[...] = lax.fori_loop(0, tiles // unroll, add, acc_ref[...])


def aggregate_tiles(rows, cols, feat, adj, nrb, steps=8, unroll=12):
    count, side, _ = adj.shape
    width = feat.shape[1]
    return pl.pallas_call(
        functools.partial(aggregate_body, unroll),
        out_shape=jax.ShapeDtypeStruct((nrb, width, side), BF),
        grid_spec=pltpu.PrefetchScalarGridSpec(
            num_scalar_prefetch=2,
            grid=(steps,),
            in_specs=[
                pl.BlockSpec(feat.shape, lambda i, a, b: (0, 0, 0), pipeline_mode=pl.Buffered(1)),
                pl.BlockSpec((count // steps, side, side), lambda i, a, b: (i, 0, 0)),
            ],
            out_specs=pl.BlockSpec((nrb, width, side), lambda i, a, b: (0, 0, 0)),
            scratch_shapes=[
                pltpu.VMEM((width, side), F32),
                pltpu.VMEM((count // steps, width, side), F32),
            ],
        ),
        compiler_params=pltpu.CompilerParams(
            vmem_limit_bytes=56 * MIB, dimension_semantics=("arbitrary",)
        ),
        cost_estimate=pl.CostEstimate(
            flops=2 * count * width * side * side,
            transcendentals=0,
            bytes_accessed=2 * (feat.size + adj.size + nrb * width * side),
        ),
        name="aggregate_tiles",
    )(rows, cols, feat, adj)


def stack_channels(own_ref, comb_ref):
    sources, own, width, side = own_ref.shape
    for r in range(own):
        comb_ref[:, pl.ds(r * side, side)] = own_ref[:, r].reshape(sources * width, side)


def dense_self_body(self_ref, weight_ref, bias_ref, comb_ref, pre_ref):
    stack_channels(self_ref, comb_ref)
    half, nodes = comb_ref.shape
    chunk = nodes // 2
    for m in range(2):
        rows = pl.ds(m * chunk, chunk)
        pre = lax.dot_general(
            comb_ref[:, rows], weight_ref[:half, :], (((0,), (0,)), ((), ())), preferred_element_type=F32
        )
        pre_ref[rows, :] = pre + bias_ref[...]


def dense_self(own_self, weight, bias):
    sources, own, width, side = own_self.shape
    vmem = pl.BlockSpec(memory_space=pltpu.VMEM)
    return pl.pallas_call(
        dense_self_body,
        out_shape=(
            pltpu.HBM((sources * width, own * side), BF),
            pltpu.HBM((own * side, weight.shape[1]), F32),
        ),
        in_specs=[vmem] * 3,
        out_specs=(vmem,) * 2,
        compiler_params=pltpu.CompilerParams(vmem_limit_bytes=56 * MIB),
        name="dense_self",
    )(in_vmem(own_self), in_hbm(weight), in_hbm(bias))


def dense_rest_body(
    core_ref, agg_ref, comb_self_hbm, pre_hbm, weight_hbm, cot_hbm,
    hidden_hbm, comb_ref, grad_ref, send_ref,
    self_rows_ref, pre_ref, weight_ref, cot_ref, hidden_ref, sem,
):
    half, nodes = comb_ref.shape
    sources = [
        (weight_hbm.at[pl.ds(half, half)], weight_ref),
        (pre_hbm, pre_ref),
        (cot_hbm, cot_ref),
    ]
    loads = [pltpu.make_async_copy(a, b, sem.at[i]) for i, (a, b) in enumerate(sources)]
    for load in loads:
        load.start()
    dest = 1 - core_ref[0]
    load_rows(dest, comb_self_hbm, self_rows_ref, sem.at[3])
    stack_channels(agg_ref, comb_ref)
    loads[0].wait()
    part = lax.dot_general(
        comb_ref[...], weight_ref[...], (((0,), (0,)), ((), ())), preferred_element_type=F32
    )
    loads[1].wait()
    loads[2].wait()
    pre = pre_ref[...] + part
    decay = jnp.exp(jnp.minimum(pre, 0.0))
    hidden_ref[...] = jnp.where(pre > 0, pre, decay - 1.0).astype(BF)
    grad_ref[...] = (cot_ref[...].astype(F32) * decay).astype(BF)
    store = pltpu.make_async_copy(hidden_ref, hidden_hbm, sem.at[4])
    store.start()
    pltpu.make_async_copy(comb_self_hbm.at[pl.ds(0, half // 2)], self_rows_ref, sem.at[3]).wait()
    weight_terms(dest, self_rows_ref, comb_ref, grad_ref, send_ref)
    store.wait()


def load_rows(dest, comb_hbm, rows_ref, sem):
    share = comb_hbm.shape[0] // 16
    for b in range(8):
        rows = pl.ds(pl.multiple_of((2 * b + dest) * share, share), share)
        pltpu.make_async_copy(comb_hbm.at[rows], rows_ref.at[pl.ds(b * share, share)], sem).start()


def weight_terms(dest, self_rows_ref, comb_ref, grad_ref, out_ref):
    blocks, share, hid = out_ref.shape
    lhs = jnp.concatenate(
        [self_rows_ref[...]]
        + [
            comb_ref[pl.ds(pl.multiple_of((2 * b + dest) * share, share), share), :]
            for b in range(blocks // 2)
        ],
        axis=0,
    )
    width = hid // 4
    for n in range(4):
        cols = pl.ds(n * width, width)
        total = jnp.dot(lhs, grad_ref[:, cols], preferred_element_type=F32)
        out_ref[:, :, cols] = total.reshape(blocks, share, width).astype(out_ref.dtype)


def pieces_of(half, hid):
    return (16, half // 16, hid)


def dense_rest(core, own_agg, comb_self, pre, weight, cot):
    nodes, hid = cot.shape
    half = comb_self.shape[0]
    vmem = pl.BlockSpec(memory_space=pltpu.VMEM)
    return pl.pallas_call(
        dense_rest_body,
        out_shape=(
            pltpu.HBM((nodes, hid), BF),
            pltpu.VMEM((half, nodes), BF),
            pltpu.VMEM((nodes, hid), BF),
            pltpu.VMEM(pieces_of(half, hid), BF),
        ),
        in_specs=[pl.BlockSpec(memory_space=pltpu.SMEM), vmem]
        + [pl.BlockSpec(memory_space=pl.ANY)] * 4,
        out_specs=(pl.BlockSpec(memory_space=pl.ANY),) + (vmem,) * 3,
        scratch_shapes=[
            pltpu.VMEM((half // 2, nodes), BF),
            pltpu.VMEM((nodes, hid), F32),
            pltpu.VMEM((half, hid), BF),
            pltpu.VMEM((nodes, hid), BF),
            pltpu.VMEM((nodes, hid), BF),
            pltpu.SemaphoreType.DMA((5,)),
        ],
        compiler_params=pltpu.CompilerParams(vmem_limit_bytes=24 * MIB),
        name="dense_rest",
    )(core, in_vmem(own_agg), *map(in_hbm, (comb_self, pre, weight, cot)))


def dense_keep_body(core_ref, comb_self_hbm, comb_ref, grad_ref, keep_ref, self_rows_ref, sem):
    load_rows(core_ref[0], comb_self_hbm, self_rows_ref, sem)
    count = self_rows_ref.shape[0]
    pltpu.make_async_copy(comb_self_hbm.at[pl.ds(0, count)], self_rows_ref, sem).wait()
    weight_terms(core_ref[0], self_rows_ref, comb_ref, grad_ref, keep_ref)


def dense_keep(core, comb_self, comb_agg, grad):
    half, nodes = comb_self.shape
    hid = grad.shape[1]
    vmem = pl.BlockSpec(memory_space=pltpu.VMEM)
    return pl.pallas_call(
        dense_keep_body,
        out_shape=pltpu.VMEM(pieces_of(half, hid), F32),
        in_specs=[pl.BlockSpec(memory_space=pltpu.SMEM), pl.BlockSpec(memory_space=pl.ANY), vmem, vmem],
        out_specs=vmem,
        scratch_shapes=[pltpu.VMEM((half // 2, nodes), BF), pltpu.SemaphoreType.DMA(())],
        compiler_params=pltpu.CompilerParams(vmem_limit_bytes=16 * MIB),
        name="dense_keep",
    )(core, in_hbm(comb_self), in_vmem(comb_agg), in_vmem(grad))


def sum_pieces_body(pieces_ref, sum_ref):
    sum_ref[...] = jnp.sum(pieces_ref[...].astype(F32), axis=0).astype(BF)


def sum_pieces(pieces):
    vmem = pl.BlockSpec(memory_space=pltpu.VMEM)
    return pl.pallas_call(
        sum_pieces_body,
        out_shape=pltpu.VMEM(pieces.shape[1:], BF),
        in_specs=[vmem],
        out_specs=vmem,
        compiler_params=pltpu.CompilerParams(vmem_limit_bytes=16 * MIB),
        name="sum_pieces",
    )(in_vmem(pieces))


def shift(value, axis, k):
    return lax.ppermute(value, axis, [(i, (i + k) % 4) for i in range(4)])


FEAT = ("x", "y", "core")


def per_device(
    features, adj_tiles, tile_rows, tile_cols, self_blocks, weight, proj_bias, cotangent
):
    feat = features[0]
    width, side = feat.shape[1:]
    nrb = self_blocks.shape[1]
    mine = gather_self(self_blocks, feat)
    feat, mine = lax.optimization_barrier((feat, mine))
    own_self = lax.all_to_all(mine, FEAT, 0, 0, tiled=True)
    agg = aggregate_tiles(tile_rows, tile_cols, feat, adj_tiles[0], nrb)
    own_agg = lax.all_to_all(agg, FEAT, 0, 0, tiled=True)
    shape = (32, nrb // 32, width, side)
    comb_self, pre = dense_self(own_self.reshape(shape), weight, proj_bias[None])
    core = lax.axis_index("core").astype(jnp.int32).reshape(1)
    hidden, comb_agg, grad, send = dense_rest(
        core, own_agg.reshape(shape), comb_self, pre, weight, cotangent[0]
    )
    other = lax.ppermute(send, "core", [(0, 1), (1, 0)])
    keep = dense_keep(core, comb_self, comb_agg, grad)
    pair = (keep + other.astype(F32)).astype(BF)
    pieces = lax.all_to_all(pair, ("x", "y"), 0, 0, tiled=True)
    mine = sum_pieces(pieces)
    n1, n2, n3 = (shift(mine, "grp", -k).astype(F32) for k in (1, 2, 3))
    odd = lax.axis_index("grp") % 2 == 1
    total = (mine.astype(F32) + jnp.where(odd, n3, n1)) + (n2 + jnp.where(odd, n1, n3))
    return hidden[None], total


def solution(mesh):
    names = ("grp", "x", "y", "core")
    fine = Mesh(mesh.devices.reshape(4, 4, 4, 2), names)
    return jax.shard_map(
        per_device,
        mesh=fine,
        in_specs=(
            P("grp", None, FEAT, None),
            P("grp", None, None, None),
            P("grp", None),
            P("grp", None),
            P("grp", None),
            P(),
            P(),
            P("grp", FEAT, None),
        ),
        out_specs=(P("grp", FEAT, None), P(FEAT, None)),
        check_vma=False,
    )
```
